128 devices in a mesh: dp: 16 (over y, z), head: 4 (over x_lo, core), group: 2 (over x_hi).
Axes of the slice: x: 4 (x_hi: 2, x_lo: 2; x = x_hi * 2 + x_lo), y: 4, z: 4, core: 2. Of those that a mesh axis runs over, the one named last changes fastest.
Arguments:
- tokens: bfloat16 [8192, 2048], P(('dp', 'head')), may hold values from -6 to 6
- grad_out: bfloat16 [8192, 2048], P(('dp', 'head')), may hold values from -6 to 6
- w_qkv: bfloat16 [3, 2048, 1024], P(None, None, ('head', 'group')), may hold values from -4 to 4
- w_attn_out: bfloat16 [1024, 2048], P(('head', 'group')), may hold values from -0.1875 to 0.1875
- gain_attn: float32 [2048], replicated, may hold values from 0.25 to 1.75
- gain_ffn: float32 [2048], replicated, may hold values from 0.25 to 1.75
- w_gate_up: bfloat16 [64, 2, 2048, 1408], P(('dp', 'head'), None, None, 'group'), may hold values from -0.125 to 0.125
- w_down: bfloat16 [64, 1408, 2048], P(('dp', 'head'), 'group'), may hold values from -0.15625 to 0.15625
- expert_ids: int32 [8192, 2], P(('dp', 'head')), may hold values from 0 to 63, all different within a row; in each aligned block of 128 rows (0 to 127, 128 to 255, ...) at most 5 rows name the same one
- gates: float32 [8192, 2], P(('dp', 'head')), may hold values from 0.05 to 0.5
Outputs:
- grad_tokens: bfloat16 [8192, 2048], P(('dp', 'head'))
- grad_qkv: float32 [3, 2048, 1024], P(None, 'dp', ('head', 'group'))
- grad_attn_out: float32 [1024, 2048], P(('head', 'group'), 'dp')
- grad_gate_up: bfloat16 [64, 2, 2048, 1408], P(('dp', 'head'), None, None, 'group')
- grad_down: bfloat16 [64, 1408, 2048], P(('dp', 'head'), 'group')
The draws below stay inside these ranges and needn't reach their ends.
Inputs may be any that keep to these rules, and one draw needn't show every extreme that they name: `expert_ids`: each row names 2 different experts; in each aligned block of 128 rows no expert is named by more than 5 rows.
All inputs are finite; a program needn't handle non-finite values.
Results may differ from the reference program's by a relative error of at most 0.012.
Values may be sent and summed in bfloat16 or wider, within the bound.
No kernel may reach another device: no remote copies, remote signals or barrier semaphores. Data moves between devices by JAX's collectives and lax.ppermute only.
A program may use at most 128 MiB of HBM per device.

```python
import math
import jax
import jax.numpy as jnp
import numpy as np
from jax import lax

D = 2048
H = 8
HD = 128
FF = 1408
TOP = 2
SEQ = 512
TOKENS = 8192
ROWS_DEV = 128
EXPERTS = 64
CAP = 5
N_DP = 16


def draw_w_qkv(key, part):
    key_base = jax.random.fold_in(key, 11)
    spread = D ** (-0.5)
    values = jax.random.normal(key_base, (3, D, H * HD), jnp.float32) * spread
    return jnp.clip(values, -4.0, 4.0).astype(jnp.bfloat16)


def shard_levels(own_key, shape, split, smallest, high):
    factor_of, own = 1.0, jax.random.fold_in(own_key, 6)
    for dim, blocks in split:
        steps = jnp.exp(jax.random.uniform(jax.random.fold_in(own, dim), (blocks,), jnp.float32, smallest / len(split), high / len(split)))
        factor_of = factor_of * jnp.repeat(steps, shape[dim] // blocks).reshape([-1 if axis == dim else 1 for axis in range(len(shape))])
    return factor_of


def deal_out(own_key, own, number, rows, amount, top, limit, skew):
    order = jax.random.permutation(own_key, amount)
    packed, ordinary = portions_of(amount, rows * top, limit, skew, True), portions_of(amount, rows * top, limit, skew, False)
    places = jnp.arange(amount)

    def named(lengths, offset_by):
        used = int((lengths > 0).sum())
        fixed = max(1, used // 4)
        passed = fixed + (places - fixed + offset_by * (used - fixed)) % max(1, amount - fixed)
        return jnp.zeros((amount,), jnp.int32).at[order[jnp.where(places < fixed, places, passed)]].set(jnp.asarray(lengths, jnp.int32))

    lengths = jnp.where(number % 4 == 0, named(packed, number // 4), named(ordinary, number - number // 4 - 1))
    mixed = jax.random.permutation(jax.random.fold_in(own, 3), amount)
    giver, taker = mixed[0:amount // 2 * 2:2], mixed[1:amount // 2 * 2:2]
    slack = jnp.minimum(lengths[giver] - 1, limit - lengths[taker]) // 2
    slack = jnp.where((giver == order[0]) | (taker == order[0]) | (lengths[taker] == 0), 0, jnp.maximum(slack, 0))
    passed = jax.random.randint(jax.random.fold_in(own, 4), (amount // 2,), 0, 1 << 20) % (slack + 1)
    lengths = lengths.at[giver].add(-passed).at[taker].add(passed)
    items = jnp.searchsorted(jnp.cumsum(lengths), jnp.arange(rows * top), side="right").astype(jnp.int32)
    table = items.reshape(top, rows).T
    table = table[jax.random.permutation(jax.random.fold_in(own, 1), rows)]
    offset_by = jax.random.randint(jax.random.fold_in(own, 2), (rows, 1), 0, top)
    return jnp.take_along_axis(table, (jnp.arange(top)[None, :] + offset_by) % top, axis=1)


def portions_of(amount, total, limit, lean, full):
    weights = [(1 << 20) // math.isqrt(grade ** lean) + 1 for grade in range(1, amount + 1)]
    largest = limit if full else min(limit, max(-(-total // amount), total * weights[0] // sum(weights)))
    least = 1 if total - largest >= amount - 1 else 0
    counts, spare = [largest] + [least] * (amount - 1), total - largest - least * (amount - 1)
    while spare > 0:
        free = [i for i in range(1, amount) if counts[i] < largest] or [i for i in range(1, amount) if counts[i] < limit]
        pool, budget = sum([weights[i] for i in free]), spare
        for i in free:
            addition = min(limit - counts[i], max(1, budget * weights[i] // pool), spare)
            counts[i] = counts[i] + addition
            spare = spare - addition
    return np.array(counts)


def normal_values(stream_key, dims, deviation, most, shards=(), held_as=jnp.bfloat16):
    level = shard_levels(stream_key, dims, shards, -0.22, 0.18) if shards else 1.0
    values = jax.random.normal(stream_key, dims, jnp.float32) * deviation * level
    return jnp.minimum(jnp.maximum(values, -most), most).astype(held_as)


def setup_inputs(seed: int = 0) -> dict:
    keys = jax.random.split(jax.random.key(seed), 11)
    tokens = normal_values(keys[0], (TOKENS, D), 1.0, 6.0, ((0, 64),))
    grad_out = normal_values(keys[1], (TOKENS, D), 1.0, 6.0, ((0, 64),))
    w_qkv = draw_w_qkv(jax.random.fold_in(keys[10], 71), 0)
    w_attn_out = normal_values(keys[3], (H * HD, D), (H * HD) ** -0.5, 0.1875, ((0, 8),))
    gain_attn = jnp.clip(1.0 + 0.15 * jax.random.normal(keys[4], (D,), jnp.float32), 0.25, 1.75)
    gain_ffn = jnp.clip(1.0 + 0.15 * jax.random.normal(keys[5], (D,), jnp.float32), 0.25, 1.75)
    w_gate_up = normal_values(keys[6], (EXPERTS, 2, D, FF), D ** -0.5, 0.125, ((0, 64), (3, 2)))
    w_down = normal_values(keys[7], (EXPERTS, FF, D), FF ** -0.5, 0.15625, ((0, 64), (1, 2)))
    expert_ids_keys = jax.random.split(jax.random.fold_in(keys[8], 1), TOKENS // ROWS_DEV)
    expert_ids_turns = jax.random.permutation(jax.random.fold_in(keys[8], 3), TOKENS // ROWS_DEV)
    expert_ids = jax.vmap(lambda own, number: deal_out(jax.random.fold_in(keys[8], 2), own, number, ROWS_DEV, EXPERTS, TOP, CAP, 2))(expert_ids_keys, expert_ids_turns).reshape((TOKENS, TOP))
    gates = jnp.clip(jnp.exp(math.log(0.5) - 2.3025851 * jax.random.uniform(keys[9], (TOKENS, TOP), jnp.float32) ** shard_levels(keys[9], (TOKENS, TOP), ((0, 64),), -0.2, 0.2)), 0.05, 0.5)
    return {"tokens": tokens, "grad_out": grad_out, "w_qkv": w_qkv, "w_attn_out": w_attn_out, "gain_attn": gain_attn, "gain_ffn": gain_ffn, "w_gate_up": w_gate_up, "w_down": w_down, "expert_ids": expert_ids, "gates": gates}


epsilon = 1e-06

def inverse_rms(values):
    return lax.rsqrt(lax.optimization_barrier(jnp.mean(values * values, axis=-1, keepdims=True)) + epsilon)

def norm_backward(values, scaling, gain, upstream):
    weighted = upstream * gain
    normed = values * scaling
    return scaling * (weighted - normed * lax.optimization_barrier(jnp.mean(weighted * normed, axis=-1, keepdims=True)))

def attention_probs(query_heads, key_heads):
    length = query_heads.shape[0]
    scores = jnp.einsum('qhd,khd->hqk', query_heads.astype(jnp.float32), key_heads.astype(jnp.float32)) * HD ** (-0.5)
    row_pos = lax.broadcasted_iota(jnp.int32, (length, length), 0)
    col_pos = lax.broadcasted_iota(jnp.int32, (length, length), 1)
    scores = jnp.where((col_pos <= row_pos)[None], scores, -1e+30)
    maxima = lax.optimization_barrier(jnp.max(scores, axis=-1, keepdims=True))
    powered = jnp.exp(scores - maxima)
    return powered / lax.optimization_barrier(jnp.sum(powered, axis=-1, keepdims=True))

def attention_forward(bundle):
    query_heads, key_heads, value_heads = bundle
    chances = attention_probs(query_heads, key_heads)
    weights_b = chances.astype(jnp.bfloat16)
    return jnp.einsum('hqk,khd->qhd', weights_b.astype(jnp.float32), value_heads.astype(jnp.float32)).astype(jnp.bfloat16)

def attention_backward(bundle):
    query_heads, key_heads, value_heads, grad_heads = bundle
    chances = attention_probs(query_heads, key_heads)
    weights_b = chances.astype(jnp.bfloat16)
    grad_f = grad_heads.astype(jnp.float32)
    grad_weights = jnp.einsum('qhd,khd->hqk', grad_f, value_heads.astype(jnp.float32))
    grad_values = jnp.einsum('hqk,qhd->khd', weights_b.astype(jnp.float32), grad_f).astype(jnp.bfloat16)
    row_total = lax.optimization_barrier(jnp.sum(chances * grad_weights, axis=-1, keepdims=True))
    grad_scores = (chances * (grad_weights - row_total) * HD ** (-0.5)).astype(jnp.bfloat16)
    grad_queries = jnp.einsum('hqk,khd->qhd', grad_scores.astype(jnp.float32), key_heads.astype(jnp.float32)).astype(jnp.bfloat16)
    grad_keys = jnp.einsum('hqk,qhd->khd', grad_scores.astype(jnp.float32), query_heads.astype(jnp.float32)).astype(jnp.bfloat16)
    return jnp.stack([grad_queries, grad_keys, grad_values])

def reference(tokens, grad_out, w_qkv, w_attn_out, gain_attn, gain_ffn, w_gate_up, w_down, expert_ids, gates):
    tokens_f = tokens.astype(jnp.float32)
    scale_one = inverse_rms(tokens_f)
    normed_one = (tokens_f * scale_one * gain_attn).astype(jnp.bfloat16)
    projected = jnp.stack([jnp.dot(normed_one, w_qkv[which], preferred_element_type=jnp.float32) for which in range(3)]).astype(jnp.bfloat16)
    split_heads = projected.reshape(3, N_DP, SEQ, H, HD)
    mixed = lax.map(attention_forward, (split_heads[0], split_heads[1], split_heads[2]))
    mixed_flat = mixed.reshape(TOKENS, H * HD)
    attn_sum = jnp.dot(mixed_flat, w_attn_out, preferred_element_type=jnp.float32)
    hidden = (tokens_f + attn_sum).astype(jnp.bfloat16)
    hidden_f = hidden.astype(jnp.float32)
    scale_two = inverse_rms(hidden_f)
    normed_two = (hidden_f * scale_two * gain_ffn).astype(jnp.bfloat16)
    grad_f = grad_out.astype(jnp.float32)
    blocks = TOKENS // ROWS_DEV
    flat_ids = expert_ids.reshape(blocks, ROWS_DEV * TOP).astype(jnp.int32)
    onehot = (flat_ids[:, :, None] == jnp.arange(EXPERTS, dtype=jnp.int32)[None, None, :]).astype(jnp.int32)
    earlier = jnp.cumsum(onehot, axis=1) - onehot
    slot_ids = lax.optimization_barrier(jnp.sum(onehot * earlier, axis=2)).astype(jnp.int32)
    token_ids = jnp.broadcast_to(jnp.arange(TOKENS, dtype=jnp.int32).reshape(blocks, ROWS_DEV, 1), (blocks, ROWS_DEV, TOP)).reshape(blocks, ROWS_DEV * TOP)
    block_ids = jnp.broadcast_to(jnp.arange(blocks, dtype=jnp.int32)[:, None], (blocks, ROWS_DEV * TOP))
    table = jnp.full((EXPERTS, blocks, CAP), TOKENS, jnp.int32).at[flat_ids, block_ids, slot_ids].set(token_ids)
    gate_table = jnp.zeros((EXPERTS, blocks, CAP), jnp.float32).at[flat_ids, block_ids, slot_ids].set(gates.reshape(blocks, ROWS_DEV * TOP))
    normed_pad = jnp.concatenate([normed_two, jnp.zeros((1, D), jnp.bfloat16)], axis=0)
    grad_pad = jnp.concatenate([grad_out, jnp.zeros((1, D), jnp.bfloat16)], axis=0)

    def expert_grads(bundle):
        token_index, gate_vals, pair_w, down_w = bundle
        flat_index = token_index.reshape(-1)
        in_rows = normed_pad[flat_index]
        in_grads = (gate_vals.reshape(-1, 1) * grad_pad[flat_index].astype(jnp.float32)).astype(jnp.bfloat16)
        gate_pre = jnp.dot(in_rows, pair_w[0], preferred_element_type=jnp.float32)
        up_pre = jnp.dot(in_rows, pair_w[1], preferred_element_type=jnp.float32)
        sigma = jax.nn.sigmoid(gate_pre)
        active = gate_pre * sigma
        product = (active * up_pre).astype(jnp.bfloat16)
        upstream = jnp.dot(in_grads, down_w.T, preferred_element_type=jnp.float32)
        grad_down_e = jnp.dot(product.T, in_grads, preferred_element_type=jnp.float32).astype(jnp.bfloat16)
        grad_gate = (upstream * up_pre * sigma * (1.0 + gate_pre * (1.0 - sigma))).astype(jnp.bfloat16)
        grad_up = (upstream * active).astype(jnp.bfloat16)
        grad_pair = jnp.stack([jnp.dot(in_rows.T, grad_gate, preferred_element_type=jnp.float32), jnp.dot(in_rows.T, grad_up, preferred_element_type=jnp.float32)]).astype(jnp.bfloat16)
        returned = (jnp.dot(grad_gate, pair_w[0].T, preferred_element_type=jnp.float32) + jnp.dot(grad_up, pair_w[1].T, preferred_element_type=jnp.float32)).astype(jnp.bfloat16)
        return (grad_pair, grad_down_e, returned)
    grad_gate_up, grad_down, returned = lax.map(expert_grads, (table, gate_table, w_gate_up, w_down))
    grad_normed = jnp.zeros((TOKENS + 1, D), jnp.float32).at[table.reshape(-1)].add(returned.reshape(-1, D).astype(jnp.float32))[:TOKENS]
    grad_hidden = grad_f + norm_backward(hidden_f, scale_two, gain_ffn, grad_normed)
    grad_hidden_b = grad_hidden.astype(jnp.bfloat16)
    grad_mixed = jnp.dot(grad_hidden_b, w_attn_out.T, preferred_element_type=jnp.float32).astype(jnp.bfloat16)
    grad_attn_out = jnp.dot(mixed_flat.T, grad_hidden_b, preferred_element_type=jnp.float32)
    grad_heads = grad_mixed.reshape(N_DP, SEQ, H, HD)
    grad_acts = lax.map(attention_backward, (split_heads[0], split_heads[1], split_heads[2], grad_heads))
    grad_acts = jnp.moveaxis(grad_acts, 1, 0).reshape(3, TOKENS, H * HD)
    grad_qkv = jnp.stack([jnp.dot(normed_one.T, grad_acts[which], preferred_element_type=jnp.float32) for which in range(3)])
    grad_normed_one = jnp.dot(grad_acts[0], w_qkv[0].T, preferred_element_type=jnp.float32)
    grad_normed_one = grad_normed_one + jnp.dot(grad_acts[1], w_qkv[1].T, preferred_element_type=jnp.float32)
    grad_normed_one = grad_normed_one + jnp.dot(grad_acts[2], w_qkv[2].T, preferred_element_type=jnp.float32)
    grad_tokens = (grad_hidden + norm_backward(tokens_f, scale_one, gain_attn, grad_normed_one)).astype(jnp.bfloat16)
    return (grad_tokens, grad_qkv, grad_attn_out, grad_gate_up, grad_down)
```

```python
import jax
import jax.numpy as jnp
from jax import lax
from jax.sharding import PartitionSpec as P

HD = 128
BF = jnp.bfloat16
F32 = jnp.float32
ALL = ("dp", "head", "group")
HG = ("head", "group")

epsilon = 1e-06


def inverse_rms(values):
    return lax.rsqrt(jnp.mean(values * values, axis=-1, keepdims=True) + epsilon)


def norm_backward(values, scaling, gain, upstream):
    weighted = upstream * gain
    normed = values * scaling
    return scaling * (weighted - normed * jnp.mean(weighted * normed, axis=-1, keepdims=True))


def swap(x, head_bits, group_bit):
    flip = head_bits * 2 + group_bit
    return lax.ppermute(x, HG, [(i, i ^ flip) for i in range(8)])


def dot(a, b, dims=((1,), (0,))):
    return lax.dot_general(a, b, (dims, ((), ())), preferred_element_type=F32)


def body(
    tokens, grad_out, w_qkv, w_attn_out, gain_attn, gain_ffn, w_gate_up, w_down, expert_ids, gates
):
    rows, width = tokens.shape
    half = width // 2
    me_head = lax.axis_index("head")
    me_group = lax.axis_index("group")
    tok_core = swap(tokens, 1, 0)
    tok_far = swap(tokens, 2, 0)
    tok_far_core = swap(tok_far, 1, 0)

    top_count = expert_ids.shape[1]
    owners = lax.axis_size("dp") * lax.axis_size("head")
    expert_count = owners
    capacity = 5
    slots = expert_count * capacity
    flat_ids = expert_ids.reshape(-1)
    onehot = (flat_ids[:, None] == lax.iota(jnp.int32, expert_count)[None, :]).astype(jnp.int32)
    earlier = jnp.cumsum(onehot, axis=0) - onehot
    slot_ids = jnp.sum(onehot * earlier, axis=1)
    targets = (flat_ids * capacity + slot_ids).reshape(rows, top_count)
    slot_iota = lax.iota(jnp.int32, slots)[:, None]
    match0 = slot_iota == targets[None, :, 0]
    match1 = slot_iota == targets[None, :, 1]
    picker = (match0 | match1).astype(BF)
    slot_gate = jnp.sum(
        jnp.where(match0, gates[None, :, 0], 0.0) + jnp.where(match1, gates[None, :, 1], 0.0),
        axis=1,
        keepdims=True,
    )

    def send_out(chosen):
        block = chosen.reshape(expert_count, 1, capacity * half // 128, 128)
        block = jnp.broadcast_to(block, (expert_count, 2, capacity * half // 128, 128))
        got = lax.all_to_all(block.reshape(2 * expert_count, -1, 128), ALL, 0, 0, tiled=True)
        got = got.reshape(expert_count, 2, capacity, half).transpose(0, 2, 1, 3)
        return got.reshape(slots, width)

    grad_half = lax.dynamic_slice_in_dim(grad_out, me_group * half, half, axis=1)
    in_grads = send_out((slot_gate * dot(picker, grad_half)).astype(BF))

    w_pair = w_attn_out.reshape(HD, 2, half)
    w_mine = lax.dynamic_index_in_dim(w_pair, me_group, 1, keepdims=False)
    w_other = lax.dynamic_index_in_dim(w_pair, 1 - me_group, 1, keepdims=False)
    w_same = [w_attn_out, None, swap(w_attn_out, 2, 0), None]
    w_cross = [swap(w_other, 0, 1), None, swap(w_other, 2, 1), None]
    for k in (0, 2):
        w_same[k + 1] = swap(w_same[k], 1, 0)
        w_cross[k + 1] = swap(w_cross[k], 1, 0)

    tok_all = jnp.concatenate([tokens, tok_core, tok_far, tok_far_core], axis=0)
    tok_all_f = tok_all.astype(F32)
    normed_all = (tok_all_f * inverse_rms(tok_all_f) * gain_attn).astype(BF)
    proj = [dot(normed_all, w_qkv[i]).astype(BF) for i in range(3)]
    query, key, value = proj
    length = 4 * rows
    index = lax.iota(jnp.int32, length)
    place = ((index // rows) ^ me_head) * rows + index % rows
    scores = dot(query, key, ((1,), (1,))) * HD ** (-0.5)
    scores = jnp.where(place[None, :] <= place[:, None], scores, -1e30)
    powered = jnp.exp(scores - jnp.max(scores, axis=-1, keepdims=True))
    chances = powered / jnp.sum(powered, axis=-1, keepdims=True)
    weights_b = chances.astype(BF)
    mixed = dot(weights_b, value).astype(BF)

    tokens_f = tok_all_f[:rows]
    total = None
    for k in range(4):
        block = mixed[k * rows : (k + 1) * rows]
        near = block if k == 0 else swap(block, k, 0)
        cross = swap(block, k, 1)
        w_near = lax.dynamic_slice_in_dim(w_same[k], me_group * half, half, axis=1)
        part = dot(near, w_near) + dot(cross, w_cross[k])
        total = part if total is None else total + part
    hidden_half = (
        lax.dynamic_slice_in_dim(tokens, me_group * half, half, axis=1).astype(F32) + total
    ).astype(BF)
    hidden_other = swap(hidden_half, 0, 1)

    in_hidden = send_out(dot(picker, hidden_half).astype(BF))

    in_hidden_f = in_hidden.astype(F32)
    in_rows = (in_hidden_f * inverse_rms(in_hidden_f) * gain_ffn).astype(BF)
    gate_w = w_gate_up[0, 0]
    up_w = w_gate_up[0, 1]
    down_w = w_down[0]
    gate_pre = dot(in_rows, gate_w)
    up_pre = dot(in_rows, up_w)
    upstream = dot(in_grads, down_w, ((1,), (1,)))
    sigma = jax.nn.sigmoid(gate_pre)
    active = gate_pre * sigma
    grad_gate = (upstream * up_pre * sigma * (1.0 + gate_pre * (1.0 - sigma))).astype(BF)
    grad_up = (upstream * active).astype(BF)
    returned = dot(grad_gate, gate_w, ((1,), (1,))) + dot(grad_up, up_w, ((1,), (1,)))
    back = returned.astype(BF).reshape(expert_count, capacity, 2, half).transpose(0, 2, 1, 3)
    back = lax.all_to_all(
        back.reshape(2 * expert_count, capacity * half // 128, 128), ALL, 0, 0, tiled=True
    )
    back = back.reshape(expert_count, 2, capacity, half)
    product = (active * up_pre).astype(BF)
    grad_down = dot(product, in_grads, ((0,), (0,))).astype(BF)[None]
    grad_pair = jnp.stack(
        [dot(in_rows, grad_gate, ((0,), (0,))), dot(in_rows, grad_up, ((0,), (0,)))]
    ).astype(BF)[None]

    def ordered(mine, other, axis):
        first = me_group == 0
        return jnp.concatenate(
            [jnp.where(first, mine, other), jnp.where(first, other, mine)], axis=axis
        )

    normed_half = dot(picker, back[:, 0].reshape(slots, half), ((0,), (0,))) + dot(
        picker, back[:, 1].reshape(slots, half), ((0,), (0,))
    )
    normed_half = normed_half.astype(BF)
    grad_normed = ordered(normed_half, swap(normed_half, 0, 1), 1).astype(F32)
    hidden_f = ordered(hidden_half, hidden_other, 1).astype(F32)
    scale_two = inverse_rms(hidden_f)
    grad_hidden = grad_out.astype(F32) + norm_backward(hidden_f, scale_two, gain_ffn, grad_normed)
    grad_hidden_b = grad_hidden.astype(BF)

    grad_mixed = []
    for k in range(4):
        piece = dot(grad_hidden_b, w_same[k], ((1,), (1,))).astype(BF)
        grad_mixed.append(piece if k == 0 else swap(piece, k, 0))
    grad_mixed = jnp.concatenate(grad_mixed, axis=0)
    gh_core = swap(grad_hidden_b, 1, 0)
    gh_far = swap(grad_hidden_b, 2, 0)
    gh_far_core = swap(gh_far, 1, 0)
    gh_all = jnp.concatenate([grad_hidden_b, gh_core, gh_far, gh_far_core], axis=0)
    grad_out_w = dot(mixed, gh_all, ((0,), (0,)))

    grad_weights = dot(grad_mixed, value, ((1,), (1,)))
    grad_values = dot(weights_b, grad_mixed, ((0,), (0,))).astype(BF)
    row_total = jnp.sum(chances * grad_weights, axis=-1, keepdims=True)
    grad_scores = (chances * (grad_weights - row_total) * HD ** (-0.5)).astype(BF)
    grad_queries = dot(grad_scores, key).astype(BF)
    grad_keys = dot(grad_scores, query, ((0,), (0,))).astype(BF)
    grad_acts = [grad_queries, grad_keys, grad_values]

    part = sum(dot(grad_acts[i], w_qkv[i], ((1,), (1,))) for i in range(3))
    part = part.reshape(4, rows, width)
    near_sum = part[0] + swap(part[1].astype(BF), 1, 0).astype(F32)
    far_sum = part[2] + swap(part[3].astype(BF), 1, 0).astype(F32)
    small = rows // 2
    mine = lax.dynamic_slice_in_dim(near_sum, me_group * small, small, axis=0)
    near_other = lax.dynamic_slice_in_dim(near_sum, (1 - me_group) * small, small, axis=0)
    far_mine = lax.dynamic_slice_in_dim(far_sum, me_group * small, small, axis=0)
    far_other = lax.dynamic_slice_in_dim(far_sum, (1 - me_group) * small, small, axis=0)
    grad_normed_one = (
        mine
        + swap(near_other.astype(BF), 0, 1).astype(F32)
        + swap(far_mine.astype(BF), 2, 0).astype(F32)
        + swap(far_other.astype(BF), 2, 1).astype(F32)
    )

    dp_size = lax.axis_size("dp")
    piece = width // dp_size
    grad_proj = jnp.stack([dot(normed_all, g, ((0,), (0,))) for g in grad_acts])
    to_send = grad_proj.astype(BF).reshape(3, dp_size, piece, HD).transpose(1, 0, 2, 3)
    to_send = to_send.reshape(dp_size, 3 * piece, HD)
    out_send = grad_out_w.astype(BF).reshape(HD, dp_size, piece).transpose(1, 0, 2)
    both = jnp.concatenate([to_send, out_send], axis=1)
    both = lax.all_to_all(both, "dp", 0, 0, tiled=True)
    both = jnp.sum(both.astype(F32), axis=0)
    grad_proj_sum = both[: 3 * piece].reshape(3, piece, HD)
    grad_out_sum = both[3 * piece :]

    own = lax.dynamic_slice_in_dim(tokens_f, me_group * small, small, axis=0)
    own_grad = lax.dynamic_slice_in_dim(grad_hidden, me_group * small, small, axis=0)
    done = (own_grad + norm_backward(own, inverse_rms(own), gain_attn, grad_normed_one)).astype(BF)
    grad_tokens = ordered(done, swap(done, 0, 1), 0)
    return (grad_tokens, grad_proj_sum, grad_out_sum, grad_pair, grad_down)


def solution(mesh):
    return jax.shard_map(
        body,
        mesh=mesh,
        in_specs=(
            P(("dp", "head"), None),
            P(("dp", "head"), None),
            P(None, None, ("head", "group")),
            P(("head", "group"), None),
            P(),
            P(),
            P(("dp", "head"), None, None, "group"),
            P(("dp", "head"), "group", None),
            P(("dp", "head"), None),
            P(("dp", "head"), None),
        ),
        out_specs=(
            P(("dp", "head"), None),
            P(None, "dp", ("head", "group")),
            P(("head", "group"), "dp"),
            P(("dp", "head"), None, None, "group"),
            P(("dp", "head"), "group", None),
        ),
        check_vma=False,
    )
```

```python
import jax
import jax.numpy as jnp
from jax import lax
from jax.experimental import pallas as pl
from jax.experimental.pallas import tpu as pltpu
from jax.sharding import PartitionSpec as P


HD = 128
CAP = 5
BF = jnp.bfloat16
F32 = jnp.float32
ALL = ("group", "dp", "head")
HG = ("head", "group")
EPSILON = 1e-06
VMEM = pl.BlockSpec(memory_space=pltpu.VMEM)
SMEM = pl.BlockSpec(memory_space=pltpu.SMEM)
HBM = pl.BlockSpec(memory_space=pl.ANY)


def inverse_rms(values):
    return lax.rsqrt(jnp.mean(values * values, axis=-1, keepdims=True) + EPSILON)


def norm_backward(values, scaling, gain, upstream):
    weighted = upstream * gain
    normed = values * scaling
    return scaling * (weighted - normed * jnp.mean(weighted * normed, axis=-1, keepdims=True))


def dot(a, b, dims=((1,), (0,))):
    return lax.dot_general(a, b, (dims, ((), ())), preferred_element_type=F32)


def shaped(shape, dtype):
    return jax.ShapeDtypeStruct(shape, dtype)


def call(kernel, outs, specs, scratch=(), flops=0, moved=0):
    return pl.pallas_call(
        kernel,
        out_shape=outs,
        in_specs=specs,
        out_specs=jax.tree.map(lambda _: VMEM, outs),
        scratch_shapes=list(scratch),
        cost_estimate=pl.CostEstimate(flops=flops, bytes_accessed=moved, transcendentals=0),
    )


def spread(scratch, values):
    slots, wide = values.shape
    n = wide // 128
    for c in range(n):
        scratch[pl.ds(c, slots, stride=n), :] = values[:, c * 128 : (c + 1) * 128]


def targets_of(along_rows, along_cols, axis):
    rows = along_rows.shape[1]
    row_id = lax.broadcasted_iota(jnp.int32, (rows, rows), 0)
    col_id = lax.broadcasted_iota(jnp.int32, (rows, rows), 1)
    before = row_id < col_id if axis == 0 else col_id < row_id
    found = []
    for k in range(2):
        if axis == 0:
            named = along_rows[k : k + 1, :]
            same = (along_cols[:, 0:1] == named) | (along_cols[:, 1:2] == named)
        else:
            named = along_cols[:, k : k + 1]
            same = (along_rows[0:1, :] == named) | (along_rows[1:2, :] == named)
        count = jnp.sum(jnp.where(same & before, 1.0, 0.0), axis=axis, keepdims=True)
        found.append(named * CAP + count.astype(jnp.int32))
    return found


def pick_matrix(along_rows, along_cols, slots):
    rows = along_rows.shape[1]
    targets = targets_of(along_rows[...], along_cols[...], 0)
    slot = lax.broadcasted_iota(jnp.int32, (slots, rows), 0)
    return slot == targets[0], slot == targets[1]


def attention_kernel(me, t0, t1, t2, t3, gain, w, query, key, value, chances, mixed, normed):
    rows = t0.shape[0]
    for k, t in enumerate((t0, t1, t2, t3)):
        values = t[...].astype(F32)
        normed[k * rows : (k + 1) * rows, :] = (values * inverse_rms(values) * gain[...]).astype(BF)
    weights = jnp.concatenate([w[0], w[1], w[2]], axis=1)
    proj = dot(normed[...], weights).astype(BF)
    q, k, v = proj[:, :HD], proj[:, HD : 2 * HD], proj[:, 2 * HD :]
    query[...] = q
    key[...] = k
    value[...] = v
    length = 4 * rows
    scores = dot(q, k, ((1,), (1,))) * HD ** (-0.5)
    row = lax.broadcasted_iota(jnp.int32, (length, length), 0)
    col = lax.broadcasted_iota(jnp.int32, (length, length), 1)
    row = ((row // rows) ^ me[0]) * rows + row % rows
    col = ((col // rows) ^ me[0]) * rows + col % rows
    scores = jnp.where(col <= row, scores, -1e30)
    powered = jnp.exp(scores - jnp.max(scores, axis=-1, keepdims=True))
    probs = powered / jnp.sum(powered, axis=-1, keepdims=True)
    chances[...] = probs
    mixed[...] = dot(probs.astype(BF), v).astype(BF)


def attention(me, blocks, gain, w_qkv):
    rows, width = blocks[0].shape
    length = 4 * rows
    head = shaped((length, HD), BF)
    return call(
        attention_kernel,
        (head, head, head, shaped((length, length), F32), head, shaped((length, width), BF)),
        [SMEM] + [VMEM] * 6,
        flops=2 * length * (3 * width + 2 * length) * HD,
        moved=2 * length * width * 2 + 3 * width * HD * 2 + length * length * 4,
    )(me, *blocks, gain, w_qkv)


def project_kernel(me, m0, m1, m2, m3, w0, w1, w2, w3, mine, other):
    half = w0.shape[1] // 2
    total = []
    for j in range(2):
        part = None
        for m, w in ((m0, w0), (m1, w1), (m2, w2), (m3, w3)):
            term = dot(m[...], w[:, j * half : (j + 1) * half])
            part = term if part is None else part + term
        total.append(part)
    first = me[1] == 0
    mine[...] = jnp.where(first, total[0], total[1])
    other[...] = jnp.where(first, total[1], total[0]).astype(BF)


def project(me, mixed, weights):
    rows, width = mixed[0].shape[0], weights[0].shape[1]
    return call(
        project_kernel,
        (shaped((rows, width // 2), F32), shaped((rows, width // 2), BF)),
        [SMEM] + [VMEM] * 8,
        flops=8 * rows * HD * width,
        moved=8 * HD * width,
    )(me, *mixed, *weights)


def grads_kernel(me, ids, ids_t, gates, grad_out, sent, scratch):
    half = grad_out.shape[1] // 2
    slots = CAP * sent.shape[0] // (2 * CAP * half // 128)
    first, second = pick_matrix(ids_t, ids, slots)
    scale = jnp.sum(
        jnp.where(first, gates[0:1, :], 0.0) + jnp.where(second, gates[1:2, :], 0.0),
        axis=1,
        keepdims=True,
    )
    picker = (first | second).astype(BF)
    chosen = jnp.where(me[1] == 0, grad_out[:, :half], grad_out[:, half:])
    spread(scratch, dot(picker, chosen) * scale)
    tiles = scratch[...].astype(BF)
    count = tiles.shape[0]
    sent[:count, :] = tiles
    sent[count:, :] = tiles


def hidden_kernel(me, ids, ids_t, tokens, mine, other, hidden, sent, scratch):
    half = mine.shape[1]
    slots = CAP * sent.shape[0] // (2 * CAP * half // 128)
    first, second = pick_matrix(ids_t, ids, slots)
    picker = (first | second).astype(BF)
    chosen = jnp.where(me[1] == 0, tokens[:, :half], tokens[:, half:]).astype(F32)
    rows = (chosen + (mine[...] + other[...].astype(F32))).astype(BF)
    hidden[...] = rows
    spread(scratch, dot(picker, rows))
    tiles = scratch[...].astype(BF)
    count = tiles.shape[0]
    sent[:count, :] = tiles
    sent[count:, :] = tiles


def send_grads(me, ids, ids_t, gates, grad_out, experts):
    rows, width = grad_out.shape
    tiles = experts * CAP * width // 2 // 128
    return call(
        grads_kernel,
        shaped((2 * tiles, 128), BF),
        [SMEM] + [VMEM] * 4,
        [pltpu.VMEM((tiles, 128), F32)],
        flops=2 * experts * CAP * rows * width // 2,
        moved=tiles * 512,
    )(me, ids, ids_t, gates, grad_out)


def send_hidden(me, ids, ids_t, tokens, mine, other, experts):
    rows, width = tokens.shape
    tiles = experts * CAP * width // 2 // 128
    return call(
        hidden_kernel,
        (shaped((rows, width // 2), BF), shaped((2 * tiles, 128), BF)),
        [SMEM] + [VMEM] * 5,
        [pltpu.VMEM((tiles, 128), F32)],
        flops=2 * experts * CAP * rows * width // 2,
        moved=tiles * 512,
    )(me, ids, ids_t, tokens, mine, other)


def gathered(scratch, got, slots, wide):
    n = wide // 2 // 128
    tiles = slots * n
    pieces = []
    for g in range(2):
        scratch[...] = got[g * tiles : (g + 1) * tiles, :].astype(F32)
        pieces.extend(scratch[pl.ds(c, slots, stride=n), :] for c in range(n))
    return jnp.concatenate(pieces, axis=1)


def expert_kernel(
    got_hidden, got_grads, gain, w_pair, w_down, sent, in_rows, in_grads, product, gate_grad,
    up_grad, scratch, pair_ref, down_ref, sems
):
    copies = [
        pltpu.make_async_copy(w_pair.at[0, 0], pair_ref.at[0], sems.at[0]),
        pltpu.make_async_copy(w_pair.at[0, 1], pair_ref.at[1], sems.at[1]),
        pltpu.make_async_copy(w_down.at[0], down_ref, sems.at[2]),
    ]
    for copy in copies:
        copy.start()
    slots, width = in_rows.shape
    values = gathered(scratch, got_hidden, slots, width)
    in_rows[...] = (values * inverse_rms(values) * gain[...]).astype(BF)
    in_grads[...] = gathered(scratch, got_grads, slots, width).astype(BF)
    rows = in_rows[...]
    copies[0].wait()
    gate_pre = dot(rows, pair_ref[0], ((1,), (1,)))
    copies[1].wait()
    up_pre = dot(rows, pair_ref[1], ((1,), (1,)))
    copies[2].wait()
    upstream = dot(in_grads[...], down_ref[...], ((1,), (1,)))
    sigma = 1.0 / (1.0 + jnp.exp(-gate_pre))
    active = gate_pre * sigma
    product[...] = (active * up_pre).astype(BF)
    gate_grad[...] = (upstream * up_pre * sigma * (1.0 + gate_pre * (1.0 - sigma))).astype(BF)
    up_grad[...] = (upstream * active).astype(BF)
    half = width // 2
    tiles = scratch.shape[0]
    for g in range(2):
        piece = slice(g * half, (g + 1) * half)
        returned = dot(gate_grad[...], pair_ref[0, :, piece]) + dot(
            up_grad[...], pair_ref[1, :, piece]
        )
        spread(scratch, returned)
        sent[g * tiles : (g + 1) * tiles, :] = scratch[...].astype(BF)


def experts_forward(got_hidden, got_grads, gain, w_pair, w_down):
    inner, width = w_pair.shape[2:]
    tiles = got_hidden.shape[0] // 2
    slots = tiles * 256 // width
    row, unit = shaped((slots, width), BF), shaped((slots, inner), BF)
    return call(
        expert_kernel,
        (shaped((2 * tiles, 128), BF), row, row, unit, unit, unit),
        [VMEM] * 3 + [HBM] * 2,
        [
            pltpu.VMEM((tiles, 128), F32),
            pltpu.VMEM((2, inner, width), BF),
            pltpu.VMEM((inner, width), BF),
            pltpu.SemaphoreType.DMA((3,)),
        ],
        flops=10 * slots * width * inner,
        moved=6 * width * inner,
    )(got_hidden, got_grads, gain, w_pair, w_down)


def expert_grads_kernel(in_rows, in_grads, product, gate_grad, up_grad, pair, down):
    rows = in_rows[...]
    pair[0, 0] = dot(gate_grad[...], rows, ((0,), (0,))).astype(BF)
    pair[0, 1] = dot(up_grad[...], rows, ((0,), (0,))).astype(BF)
    down[0] = dot(product[...], in_grads[...], ((0,), (0,))).astype(BF)


def expert_grads(in_rows, in_grads, product, gate_grad, up_grad):
    slots, width = in_rows.shape
    inner = product.shape[1]
    parts = 4
    row = pl.BlockSpec((slots, width // parts), lambda i: (0, i))
    unit = pl.BlockSpec((slots, inner), lambda i: (0, 0))
    return pl.pallas_call(
        expert_grads_kernel,
        out_shape=(shaped((1, 2, inner, width), BF), shaped((1, inner, width), BF)),
        grid=(parts,),
        in_specs=[row, row, unit, unit, unit],
        out_specs=(
            pl.BlockSpec((1, 2, inner, width // parts), lambda i: (0, 0, 0, i)),
            pl.BlockSpec((1, inner, width // parts), lambda i: (0, 0, i)),
        ),
        cost_estimate=pl.CostEstimate(
            flops=6 * slots * width * inner, bytes_accessed=6 * width * inner, transcendentals=0
        ),
    )(in_rows, in_grads, product, gate_grad, up_grad)


def combine_kernel(ids, ids_t, got, out, scratch):
    rows, half = out.shape
    tiles = scratch.shape[0]
    n = half // 128
    slots = tiles // n
    scratch[...] = got[:tiles, :].astype(F32) + got[tiles:, :].astype(F32)
    values = jnp.concatenate(
        [scratch[pl.ds(c, slots, stride=n), :] for c in range(n)], axis=1
    ).astype(BF)
    slot = lax.broadcasted_iota(jnp.int32, (rows, slots), 1)
    targets = targets_of(ids_t[...], ids[...], 1)
    picker = ((slot == targets[0]) | (slot == targets[1])).astype(BF)
    out[...] = dot(picker, values).astype(BF)


def combine(ids, ids_t, got, half):
    rows = ids.shape[0]
    tiles = got.shape[0] // 2
    return call(
        combine_kernel,
        shaped((rows, half), BF),
        [VMEM] * 3,
        [pltpu.VMEM((tiles, 128), F32)],
        flops=2 * rows * tiles * 128,
        moved=tiles * 512,
    )(ids, ids_t, got)


def hidden_grad_kernel(
    me, grad_out, hidden_mine, hidden_other, normed_mine, normed_other, gain, w0, w1, w2, w3,
    grad, rounded, p0, p1, p2, p3
):
    first = me[1] == 0

    def whole(mine, other):
        a, b = mine[...].astype(F32), other[...].astype(F32)
        return jnp.concatenate([jnp.where(first, a, b), jnp.where(first, b, a)], axis=1)

    hidden = whole(hidden_mine, hidden_other)
    upstream = whole(normed_mine, normed_other)
    value = grad_out[...].astype(F32) + norm_backward(
        hidden, inverse_rms(hidden), gain[...], upstream
    )
    grad[...] = value
    low = value.astype(BF)
    rounded[...] = low
    for p, w in ((p0, w0), (p1, w1), (p2, w2), (p3, w3)):
        p[...] = dot(low, w[...], ((1,), (1,))).astype(BF)


def hidden_grad(me, grad_out, halves, gain, weights):
    rows, width = grad_out.shape
    piece = shaped((rows, HD), BF)
    return call(
        hidden_grad_kernel,
        (shaped((rows, width), F32), shaped((rows, width), BF), piece, piece, piece, piece),
        [SMEM] + [VMEM] * 10,
        flops=8 * rows * width * HD,
        moved=8 * HD * width + 10 * rows * width,
    )(me, grad_out, *halves, gain, *weights)


def attention_back_kernel(
    g0, g1, g2, g3, query, key, value, chances, w, acts, near, far, near_out, far_out
):
    rows = g0.shape[0]
    grad = jnp.concatenate([g0[...], g1[...], g2[...], g3[...]], axis=0)
    probs = chances[...]
    grad_weights = dot(grad, value[...], ((1,), (1,)))
    total = jnp.sum(probs * grad_weights, axis=-1, keepdims=True)
    scores = (probs * (grad_weights - total) * HD ** (-0.5)).astype(BF)
    acts[:, :HD] = dot(scores, key[...]).astype(BF)
    acts[:, HD : 2 * HD] = dot(scores, query[...], ((0,), (0,))).astype(BF)
    acts[:, 2 * HD :] = dot(probs.astype(BF), grad, ((0,), (0,))).astype(BF)
    weights = jnp.concatenate([w[0], w[1], w[2]], axis=1)
    for k, out in enumerate((near, near_out, far, far_out)):
        part = dot(acts[k * rows : (k + 1) * rows, :], weights, ((1,), (1,)))
        out[...] = part.astype(out.dtype)


def attention_back(grads, query, key, value, chances, w_qkv):
    rows = grads[0].shape[0]
    width = w_qkv.shape[1]
    length = 4 * rows
    kept, sent = shaped((rows, width), F32), shaped((rows, width), BF)
    return call(
        attention_back_kernel,
        (shaped((length, 3 * HD), BF), kept, kept, sent, sent),
        [VMEM] * 9,
        flops=2 * length * (3 * width + 4 * length) * HD,
        moved=3 * width * HD * 2 + length * length * 4 + 3 * length * width,
    )(*grads, query, key, value, chances, w_qkv)


def weight_kernel(acts, normed, mixed, g0, g1, g2, g3, sent):
    pieces = sent.shape[0]
    wide = acts.shape[1]
    left = dot(acts[...], normed[...], ((0,), (0,))).astype(BF)
    grads = jnp.concatenate([g0[...], g1[...], g2[...], g3[...]], axis=0)
    right = dot(mixed[...], grads, ((0,), (0,))).astype(BF)
    for j in range(pieces):
        sent[j, :wide, :] = left[:, j * 128 : (j + 1) * 128]
        sent[j, wide:, :] = right[:, j * 128 : (j + 1) * 128]


def weight_grads(acts, normed, mixed, grads, pieces):
    length, width = normed.shape
    return call(
        weight_kernel,
        shaped((pieces, 4 * HD, width // pieces), BF),
        [VMEM] * 7,
        flops=8 * length * width * HD,
        moved=4 * length * width + 8 * HD * width,
    )(acts, normed, mixed, *grads)


def weight_sum_kernel(got, qkv, out):
    total = jnp.sum(got[...].astype(F32), axis=0)
    for i in range(3):
        qkv[i] = total[i * HD : (i + 1) * HD, :].T
    out[...] = total[3 * HD :, :]


def weight_sum(got):
    piece = got.shape[2]
    return call(
        weight_sum_kernel,
        (shaped((3, piece, HD), F32), shaped((HD, piece), F32)),
        [VMEM],
        flops=got.size,
        moved=got.size * 2,
    )(got)


def split_kernel(me, near, near_in, far, far_in, mine, near_other, far_mine, far_other):
    small = mine.shape[0]
    here = near[...] + near_in[...].astype(F32)
    there = far[...] + far_in[...].astype(F32)
    first = me[1] == 0
    mine[...] = jnp.where(first, here[:small], here[small:])
    near_other[...] = jnp.where(first, here[small:], here[:small]).astype(BF)
    far_mine[...] = jnp.where(first, there[:small], there[small:]).astype(BF)
    far_other[...] = jnp.where(first, there[small:], there[:small]).astype(BF)


def split_sums(me, near, near_in, far, far_in):
    rows, width = near.shape
    low = shaped((rows // 2, width), BF)
    return call(
        split_kernel,
        (shaped((rows // 2, width), F32), low, low, low),
        [SMEM] + [VMEM] * 4,
        flops=4 * rows * width,
        moved=20 * rows * width,
    )(me, near, near_in, far, far_in)


def tokens_kernel(me, mine, a, b, c, tokens, grad_hidden, gain, out):
    small = mine.shape[0]
    first = me[1] == 0
    upstream = (
        mine[...] + a[...].astype(F32) + b[...].astype(F32) + c[...].astype(F32)
    )
    values = jnp.where(first, tokens[:small], tokens[small:]).astype(F32)
    before = jnp.where(first, grad_hidden[:small], grad_hidden[small:])
    back = norm_backward(values, inverse_rms(values), gain[...], upstream)
    out[...] = (before + back).astype(BF)


def tokens_grad(me, mine, arrived, tokens, grad_hidden, gain):
    small, width = mine.shape
    return call(
        tokens_kernel,
        shaped((small, width), BF),
        [SMEM] + [VMEM] * 7,
        flops=20 * small * width,
        moved=30 * small * width,
    )(me, mine, *arrived, tokens, grad_hidden, gain)


def join_kernel(me, mine, other, out):
    small = mine.shape[0]
    first = me[1] == 0
    out[:small] = jnp.where(first, mine[...], other[...])
    out[small:] = jnp.where(first, other[...], mine[...])


def join(me, mine, other):
    small, width = mine.shape
    return call(
        join_kernel,
        shaped((2 * small, width), BF),
        [SMEM] + [VMEM] * 2,
        moved=8 * small * width,
    )(me, mine, other)


def swap(x, head_bits, group_bit):
    flip = head_bits * 2 + group_bit
    return lax.ppermute(x, HG, [(i, i ^ flip) for i in range(8)])


def sequence(x):
    small = x.shape[0] // 2
    top, bottom = x[:small], x[small:]
    far = jnp.concatenate([swap(top, 2, 0), swap(bottom, 2, 1)], axis=0)
    return [x, swap(x, 1, 0), far, swap(far, 1, 0)]


def exchange(tiles):
    count = lax.axis_size(ALL)
    tiles = tiles.reshape(count, -1, 128)
    return lax.all_to_all(tiles, ALL, 0, 0, tiled=True).reshape(-1, 128)


def body(
    tokens, grad_out, w_qkv, w_attn_out, gain_attn, gain_ffn, w_gate_up, w_down, ids, gates
):
    rows, width = tokens.shape
    half = width // 2
    experts = lax.axis_size("dp") * lax.axis_size("head")
    me = jnp.stack([lax.axis_index("head"), lax.axis_index("group")]).astype(jnp.int32)
    gain_attn, gain_ffn = gain_attn[None], gain_ffn[None]
    w_pair = w_gate_up.transpose(0, 1, 3, 2)
    ids_t, gates_t = ids.T, gates.T

    blocks = sequence(tokens)
    tiles = send_grads(me, ids, ids_t, gates_t, grad_out, experts)
    got_grads = exchange(tiles)
    w_far, blocks[2] = lax.optimization_barrier((w_attn_out, blocks[2]))
    w_far = swap(w_far, 2, 0)
    weights = [w_attn_out, swap(w_attn_out, 1, 0), w_far, swap(w_far, 1, 0)]

    query, key, value, chances, mixed, normed = attention(me, blocks, gain_attn, w_qkv)
    heads = [mixed[k * rows : (k + 1) * rows] for k in range(4)]
    heads = [heads[0]] + [swap(heads[k], k, 0) for k in range(1, 4)]
    mine, other = project(me, heads, weights)
    other = swap(other, 0, 1)
    hidden, tiles = send_hidden(me, ids, ids_t, tokens, mine, other, experts)
    tiles, got_grads = lax.optimization_barrier((tiles, got_grads))
    hidden_other = swap(hidden, 0, 1)
    got_hidden = exchange(tiles)
    got_hidden, hidden_other = lax.optimization_barrier((got_hidden, hidden_other))

    tiles, *saved = experts_forward(got_hidden, got_grads, gain_ffn, w_pair, w_down)
    grad_pair, grad_down = expert_grads(*saved)
    got_back = exchange(tiles)
    got_back, grad_pair, grad_down = lax.optimization_barrier((got_back, grad_pair, grad_down))

    upstream = combine(ids, ids_t, got_back, half)
    halves = (hidden, hidden_other, upstream, swap(upstream, 0, 1))
    grad_hidden, rounded, *grads = hidden_grad(me, grad_out, halves, gain_ffn, weights)
    grads = [grads[0]] + [swap(grads[k], k, 0) for k in range(1, 4)]
    all_grads = sequence(rounded)

    acts, near, far, near_out, far_out = attention_back(grads, query, key, value, chances, w_qkv)
    near_in = swap(near_out, 1, 0)
    far_in = swap(far_out, 1, 0)
    sent = weight_grads(acts, normed, mixed, all_grads, lax.axis_size("dp"))
    got = lax.all_to_all(sent, "dp", 0, 0, tiled=True)
    mine, near_other, far_mine, far_other = split_sums(me, near, near_in, far, far_in)
    arrived = (swap(near_other, 0, 1), swap(far_mine, 2, 0), swap(far_other, 2, 1))
    done = tokens_grad(me, mine, arrived, tokens, grad_hidden, gain_attn)
    done_other = swap(done, 0, 1)
    grad_tokens = join(me, done, done_other)
    grad_qkv, grad_attn_out = weight_sum(got)
    return (grad_tokens, grad_qkv, grad_attn_out, grad_pair.transpose(0, 1, 3, 2), grad_down)


def solution(mesh):
    return jax.shard_map(
        body,
        mesh=mesh,
        in_specs=(
            P(("dp", "head"), None),
            P(("dp", "head"), None),
            P(None, None, ("head", "group")),
            P(("head", "group"), None),
            P(),
            P(),
            P(("dp", "head"), None, None, "group"),
            P(("dp", "head"), "group", None),
            P(("dp", "head"), None),
            P(("dp", "head"), None),
        ),
        out_specs=(
            P(("dp", "head"), None),
            P(None, "dp", ("head", "group")),
            P(("head", "group"), "dp"),
            P(("dp", "head"), None, None, "group"),
            P(("dp", "head"), "group", None),
        ),
        check_vma=False,
    )
```

```python
import jax
import jax.numpy as jnp
from jax import lax
from jax.experimental import pallas as pl
from jax.experimental.pallas import tpu as pltpu
from jax.sharding import PartitionSpec as P


HD = 128
CAP = 5
BF = jnp.bfloat16
F32 = jnp.float32
ALL = ("group", "dp", "head")
HG = ("head", "group")
EPSILON = 1e-06
VMEM = pl.BlockSpec(memory_space=pltpu.VMEM)
SMEM = pl.BlockSpec(memory_space=pltpu.SMEM)
HBM = pl.BlockSpec(memory_space=pl.ANY)


def inverse_rms(values):
    return lax.rsqrt(jnp.mean(values * values, axis=-1, keepdims=True) + EPSILON)


def norm_backward(values, scaling, gain, upstream):
    weighted = upstream * gain
    normed = values * scaling
    return scaling * (weighted - normed * jnp.mean(weighted * normed, axis=-1, keepdims=True))


def dot(a, b, dims=((1,), (0,))):
    return lax.dot_general(a, b, (dims, ((), ())), preferred_element_type=F32)


def shaped(shape, dtype):
    return jax.ShapeDtypeStruct(shape, dtype)


def call(kernel, outs, specs, scratch=(), flops=0, moved=0):
    return pl.pallas_call(
        kernel,
        out_shape=outs,
        in_specs=specs,
        out_specs=jax.tree.map(lambda _: VMEM, outs),
        scratch_shapes=list(scratch),
        cost_estimate=pl.CostEstimate(flops=flops, bytes_accessed=moved, transcendentals=0),
    )


def spread(scratch, values):
    slots, wide = values.shape
    n = wide // 128
    for c in range(n):
        scratch[pl.ds(c, slots, stride=n), :] = values[:, c * 128 : (c + 1) * 128]


def targets_of(along_rows, along_cols, axis):
    rows = along_rows.shape[1]
    row_id = lax.broadcasted_iota(jnp.int32, (rows, rows), 0)
    col_id = lax.broadcasted_iota(jnp.int32, (rows, rows), 1)
    before = row_id < col_id if axis == 0 else col_id < row_id
    found = []
    for k in range(2):
        if axis == 0:
            named = along_rows[k : k + 1, :]
            same = (along_cols[:, 0:1] == named) | (along_cols[:, 1:2] == named)
        else:
            named = along_cols[:, k : k + 1]
            same = (along_rows[0:1, :] == named) | (along_rows[1:2, :] == named)
        count = jnp.sum(jnp.where(same & before, 1.0, 0.0), axis=axis, keepdims=True)
        found.append(named * CAP + count.astype(jnp.int32))
    return found


def pick_matrix(along_rows, along_cols, slots):
    rows = along_rows.shape[1]
    targets = targets_of(along_rows[...], along_cols[...], 0)
    slot = lax.broadcasted_iota(jnp.int32, (slots, rows), 0)
    return slot == targets[0], slot == targets[1]


def attention_kernel(me, t0, t1, t2, t3, gain, w, query, key, value, chances, m0, m1, m2, m3, normed, held, sems):
    rows = t0.shape[0]
    copies = [
        pltpu.make_async_copy(t, held.at[k], sems.at[k]) for k, t in enumerate((t0, t1, t2, t3))
    ]
    for copy in copies:
        copy.start()
    for k, copy in enumerate(copies):
        copy.wait()
        values = held[k].astype(F32)
        normed[k * rows : (k + 1) * rows, :] = (values * inverse_rms(values) * gain[...]).astype(BF)
    weights = jnp.concatenate([w[0], w[1], w[2]], axis=1)
    proj = dot(normed[...], weights).astype(BF)
    q, k, v = proj[:, :HD], proj[:, HD : 2 * HD], proj[:, 2 * HD :]
    query[...] = q
    key[...] = k
    value[...] = v
    length = 4 * rows
    scores = dot(q, k, ((1,), (1,))) * HD ** (-0.5)
    row = lax.broadcasted_iota(jnp.int32, (length, length), 0)
    col = lax.broadcasted_iota(jnp.int32, (length, length), 1)
    row = ((row // rows) ^ me[0]) * rows + row % rows
    col = ((col // rows) ^ me[0]) * rows + col % rows
    scores = jnp.where(col <= row, scores, -1e30)
    powered = jnp.exp(scores - jnp.max(scores, axis=-1, keepdims=True))
    probs = powered / jnp.sum(powered, axis=-1, keepdims=True)
    chances[...] = probs
    mixed = dot(probs.astype(BF), v).astype(BF)
    for k, m in enumerate((m0, m1, m2, m3)):
        m[...] = mixed[k * rows : (k + 1) * rows]


def attention(me, blocks, gain, w_qkv):
    rows, width = blocks[0].shape
    length = 4 * rows
    head = shaped((length, HD), BF)
    return call(
        attention_kernel,
        (head, head, head, shaped((length, length), F32))
        + (shaped((rows, HD), BF),) * 4
        + (shaped((length, width), BF),),
        [SMEM] + [HBM] * 4 + [VMEM] * 2,
        [pltpu.VMEM((4, rows, width), BF), pltpu.SemaphoreType.DMA((4,))],
        flops=2 * length * (3 * width + 2 * length) * HD,
        moved=2 * length * width * 2 + 3 * width * HD * 2 + length * length * 4,
    )(me, *blocks, gain, w_qkv)


def project_kernel(me, m0, m1, m2, m3, w0, w1, w2, w3, mine, other):
    half = w0.shape[1] // 2
    total = []
    for j in range(2):
        part = None
        for m, w in ((m0, w0), (m1, w1), (m2, w2), (m3, w3)):
            term = dot(m[...], w[:, j * half : (j + 1) * half])
            part = term if part is None else part + term
        total.append(part)
    first = me[1] == 0
    mine[...] = jnp.where(first, total[0], total[1])
    other[...] = jnp.where(first, total[1], total[0]).astype(BF)


def project(me, mixed, weights):
    rows, width = mixed[0].shape[0], weights[0].shape[1]
    return call(
        project_kernel,
        (shaped((rows, width // 2), F32), shaped((rows, width // 2), BF)),
        [SMEM] + [VMEM] * 8,
        flops=8 * rows * HD * width,
        moved=8 * HD * width,
    )(me, *mixed, *weights)


def grads_kernel(me, ids, ids_t, gates, grad_out, sent, scratch):
    half = grad_out.shape[1] // 2
    slots = CAP * sent.shape[0] // (2 * CAP * half // 128)
    first, second = pick_matrix(ids_t, ids, slots)
    scale = jnp.sum(
        jnp.where(first, gates[0:1, :], 0.0) + jnp.where(second, gates[1:2, :], 0.0),
        axis=1,
        keepdims=True,
    )
    picker = (first | second).astype(BF)
    chosen = grad_out[:, pl.ds(pl.multiple_of(me[1] * half, half), half)]
    spread(scratch, dot(picker, chosen) * scale)
    tiles = scratch[...].astype(BF)
    count = tiles.shape[0]
    sent[:count, :] = tiles
    sent[count:, :] = tiles


def hidden_kernel(me, ids, ids_t, tokens, mine, other, hidden, sent, scratch):
    half = mine.shape[1]
    slots = CAP * sent.shape[0] // (2 * CAP * half // 128)
    first, second = pick_matrix(ids_t, ids, slots)
    picker = (first | second).astype(BF)
    chosen = tokens[:, pl.ds(pl.multiple_of(me[1] * half, half), half)].astype(F32)
    rows = (chosen + (mine[...] + other[...].astype(F32))).astype(BF)
    hidden[...] = rows
    spread(scratch, dot(picker, rows))
    tiles = scratch[...].astype(BF)
    count = tiles.shape[0]
    sent[:count, :] = tiles
    sent[count:, :] = tiles


def send_grads(me, ids, ids_t, gates, grad_out, experts):
    rows, width = grad_out.shape
    tiles = experts * CAP * width // 2 // 128
    return call(
        grads_kernel,
        shaped((2 * tiles, 128), BF),
        [SMEM] + [VMEM] * 4,
        [pltpu.VMEM((tiles, 128), F32)],
        flops=2 * experts * CAP * rows * width // 2,
        moved=tiles * 512,
    )(me, ids, ids_t, gates, grad_out)


def send_hidden(me, ids, ids_t, tokens, mine, other, experts):
    rows, width = tokens.shape
    tiles = experts * CAP * width // 2 // 128
    return call(
        hidden_kernel,
        (shaped((rows, width // 2), BF), shaped((2 * tiles, 128), BF)),
        [SMEM] + [VMEM] * 5,
        [pltpu.VMEM((tiles, 128), F32)],
        flops=2 * experts * CAP * rows * width // 2,
        moved=tiles * 512,
    )(me, ids, ids_t, tokens, mine, other)


def gathered(scratch, got, slots, wide):
    n = wide // 2 // 128
    tiles = slots * n
    pieces = []
    for g in range(2):
        scratch[...] = got[g * tiles : (g + 1) * tiles, :].astype(F32)
        pieces.extend(scratch[pl.ds(c, slots, stride=n), :] for c in range(n))
    return jnp.concatenate(pieces, axis=1)


def early_kernel(got_grads, w_down, in_grads, upstream, scratch, down_ref, sem):
    copy = pltpu.make_async_copy(w_down.at[0], down_ref, sem)
    copy.start()
    slots, width = in_grads.shape
    in_grads[...] = gathered(scratch, got_grads, slots, width).astype(BF)
    copy.wait()
    upstream[...] = dot(in_grads[...], down_ref[...], ((1,), (1,)))


def experts_early(got_grads, w_down):
    inner, width = w_down.shape[1:]
    tiles = got_grads.shape[0] // 2
    slots = tiles * 256 // width
    return call(
        early_kernel,
        (shaped((slots, width), BF), shaped((slots, inner), F32)),
        [VMEM, HBM],
        [pltpu.VMEM((tiles, 128), F32), pltpu.VMEM((inner, width), BF), pltpu.SemaphoreType.DMA],
        flops=2 * slots * width * inner,
        moved=2 * width * inner,
    )(got_grads, w_down)


def expert_kernel(
    got_hidden, upstream_ref, gain, w_pair, sent, in_rows, product, gate_grad, up_grad, scratch,
    pair_ref, sems
):
    copies = [
        pltpu.make_async_copy(w_pair.at[0, 0], pair_ref.at[0], sems.at[0]),
        pltpu.make_async_copy(w_pair.at[0, 1], pair_ref.at[1], sems.at[1]),
    ]
    for copy in copies:
        copy.start()
    slots, width = in_rows.shape
    values = gathered(scratch, got_hidden, slots, width)
    in_rows[...] = (values * inverse_rms(values) * gain[...]).astype(BF)
    rows = in_rows[...]
    copies[0].wait()
    gate_pre = dot(rows, pair_ref[0], ((1,), (1,)))
    copies[1].wait()
    up_pre = dot(rows, pair_ref[1], ((1,), (1,)))
    upstream = upstream_ref[...]
    sigma = 1.0 / (1.0 + jnp.exp(-gate_pre))
    active = gate_pre * sigma
    product[...] = (active * up_pre).astype(BF)
    gate_grad[...] = (upstream * up_pre * sigma * (1.0 + gate_pre * (1.0 - sigma))).astype(BF)
    up_grad[...] = (upstream * active).astype(BF)
    half = width // 2
    tiles = scratch.shape[0]
    for g in range(2):
        piece = slice(g * half, (g + 1) * half)
        returned = dot(gate_grad[...], pair_ref[0, :, piece]) + dot(
            up_grad[...], pair_ref[1, :, piece]
        )
        spread(scratch, returned)
        sent[g * tiles : (g + 1) * tiles, :] = scratch[...].astype(BF)


def experts_forward(got_hidden, upstream, gain, w_pair):
    inner, width = w_pair.shape[2:]
    tiles = got_hidden.shape[0] // 2
    slots = tiles * 256 // width
    row, unit = shaped((slots, width), BF), shaped((slots, inner), BF)
    return call(
        expert_kernel,
        (shaped((2 * tiles, 128), BF), row, unit, unit, unit),
        [VMEM] * 3 + [HBM],
        [
            pltpu.VMEM((tiles, 128), F32),
            pltpu.VMEM((2, inner, width), BF),
            pltpu.SemaphoreType.DMA((2,)),
        ],
        flops=8 * slots * width * inner,
        moved=4 * width * inner,
    )(got_hidden, upstream, gain, w_pair)


def expert_grads_kernel(in_rows, in_grads, product, gate_grad, up_grad, pair, down):
    rows = in_rows[...]
    pair[0, 0] = dot(gate_grad[...], rows, ((0,), (0,))).astype(BF)
    pair[0, 1] = dot(up_grad[...], rows, ((0,), (0,))).astype(BF)
    down[0] = dot(product[...], in_grads[...], ((0,), (0,))).astype(BF)


def expert_grads(in_rows, in_grads, product, gate_grad, up_grad):
    slots, width = in_rows.shape
    inner = product.shape[1]
    parts = 4
    row = pl.BlockSpec((slots, width // parts), lambda i: (0, i))
    unit = pl.BlockSpec((slots, inner), lambda i: (0, 0))
    return pl.pallas_call(
        expert_grads_kernel,
        out_shape=(shaped((1, 2, inner, width), BF), shaped((1, inner, width), BF)),
        grid=(parts,),
        in_specs=[row, row, unit, unit, unit],
        out_specs=(
            pl.BlockSpec((1, 2, inner, width // parts), lambda i: (0, 0, 0, i)),
            pl.BlockSpec((1, inner, width // parts), lambda i: (0, 0, i)),
        ),
        cost_estimate=pl.CostEstimate(
            flops=6 * slots * width * inner, bytes_accessed=6 * width * inner, transcendentals=0
        ),
    )(in_rows, in_grads, product, gate_grad, up_grad)


def combine_kernel(ids, ids_t, got, out, scratch):
    rows, half = out.shape
    tiles = scratch.shape[0]
    n = half // 128
    slots = tiles // n
    scratch[...] = got[:tiles, :].astype(F32) + got[tiles:, :].astype(F32)
    values = jnp.concatenate(
        [scratch[pl.ds(c, slots, stride=n), :] for c in range(n)], axis=1
    ).astype(BF)
    slot = lax.broadcasted_iota(jnp.int32, (rows, slots), 1)
    targets = targets_of(ids_t[...], ids[...], 1)
    picker = ((slot == targets[0]) | (slot == targets[1])).astype(BF)
    out[...] = dot(picker, values).astype(BF)


def combine(ids, ids_t, got, half):
    rows = ids.shape[0]
    tiles = got.shape[0] // 2
    return call(
        combine_kernel,
        shaped((rows, half), BF),
        [VMEM] * 3,
        [pltpu.VMEM((tiles, 128), F32)],
        flops=2 * rows * tiles * 128,
        moved=tiles * 512,
    )(ids, ids_t, got)


def hidden_grad_kernel(
    me, grad_out, hidden_mine, hidden_other, normed_mine, normed_other, gain, w0, w1, w2, w3,
    grad, rounded, top, bottom, p0, p1, p2, p3
):
    first = me[1] == 0

    def whole(mine, other):
        a, b = mine[...].astype(F32), other[...].astype(F32)
        return jnp.concatenate([jnp.where(first, a, b), jnp.where(first, b, a)], axis=1)

    hidden = whole(hidden_mine, hidden_other)
    upstream = whole(normed_mine, normed_other)
    value = grad_out[...].astype(F32) + norm_backward(
        hidden, inverse_rms(hidden), gain[...], upstream
    )
    grad[...] = value
    low = value.astype(BF)
    rounded[...] = low
    top[...] = low[: top.shape[0]]
    bottom[...] = low[top.shape[0] :]
    for p, w in ((p0, w0), (p1, w1), (p2, w2), (p3, w3)):
        p[...] = dot(low, w[...], ((1,), (1,))).astype(BF)


def hidden_grad(me, grad_out, halves, gain, weights):
    rows, width = grad_out.shape
    piece = shaped((rows, HD), BF)
    return call(
        hidden_grad_kernel,
        (shaped((rows, width), F32), shaped((rows, width), BF))
        + (shaped((rows // 2, width), BF),) * 2
        + (piece,) * 4,
        [SMEM] + [VMEM] * 10,
        flops=8 * rows * width * HD,
        moved=8 * HD * width + 10 * rows * width,
    )(me, grad_out, *halves, gain, *weights)


def attention_back_kernel(
    g0, g1, g2, g3, query, key, value, chances, w, acts, near, far, near_out, far_out
):
    rows = g0.shape[0]
    grad = jnp.concatenate([g0[...], g1[...], g2[...], g3[...]], axis=0)
    probs = chances[...]
    grad_weights = dot(grad, value[...], ((1,), (1,)))
    total = jnp.sum(probs * grad_weights, axis=-1, keepdims=True)
    scores = (probs * (grad_weights - total) * HD ** (-0.5)).astype(BF)
    acts[:, :HD] = dot(scores, key[...]).astype(BF)
    acts[:, HD : 2 * HD] = dot(scores, query[...], ((0,), (0,))).astype(BF)
    acts[:, 2 * HD :] = dot(probs.astype(BF), grad, ((0,), (0,))).astype(BF)
    weights = jnp.concatenate([w[0], w[1], w[2]], axis=1)
    for k, out in enumerate((near, near_out, far, far_out)):
        part = dot(acts[k * rows : (k + 1) * rows, :], weights, ((1,), (1,)))
        out[...] = part.astype(out.dtype)


def attention_back(grads, query, key, value, chances, w_qkv):
    rows = grads[0].shape[0]
    width = w_qkv.shape[1]
    length = 4 * rows
    kept, sent = shaped((rows, width), F32), shaped((rows, width), BF)
    return call(
        attention_back_kernel,
        (shaped((length, 3 * HD), BF), kept, kept, sent, sent),
        [VMEM] * 9,
        flops=2 * length * (3 * width + 4 * length) * HD,
        moved=3 * width * HD * 2 + length * length * 4 + 3 * length * width,
    )(*grads, query, key, value, chances, w_qkv)


def weight_kernel(acts, normed, m0, m1, m2, m3, g0, g1, g2, g3, sent):
    pieces = sent.shape[0]
    wide = acts.shape[1]
    left = dot(acts[...], normed[...], ((0,), (0,))).astype(BF)
    grads = jnp.concatenate([g0[...], g1[...], g2[...], g3[...]], axis=0)
    mixed = jnp.concatenate([m0[...], m1[...], m2[...], m3[...]], axis=0)
    right = dot(mixed, grads, ((0,), (0,))).astype(BF)
    for j in range(pieces):
        sent[j, :wide, :] = left[:, j * 128 : (j + 1) * 128]
        sent[j, wide:, :] = right[:, j * 128 : (j + 1) * 128]


def weight_grads(acts, normed, mixed, grads, pieces):
    length, width = normed.shape
    return call(
        weight_kernel,
        shaped((pieces, 4 * HD, width // pieces), BF),
        [VMEM] * 10,
        flops=8 * length * width * HD,
        moved=4 * length * width + 8 * HD * width,
    )(acts, normed, *mixed, *grads)


def weight_sum_kernel(got, qkv, out, held, sems):
    count = got.shape[0]
    copies = [pltpu.make_async_copy(got.at[j], held.at[j], sems.at[j]) for j in range(count)]
    for copy in copies:
        copy.start()
    total = None
    for j, copy in enumerate(copies):
        copy.wait()
        term = held[j].astype(F32)
        total = term if total is None else total + term
    for i in range(3):
        qkv[i] = total[i * HD : (i + 1) * HD, :].T
    out[...] = total[3 * HD :, :]


def weight_sum(got):
    piece = got.shape[2]
    return call(
        weight_sum_kernel,
        (shaped((3, piece, HD), F32), shaped((HD, piece), F32)),
        [HBM],
        [pltpu.VMEM(got.shape, BF), pltpu.SemaphoreType.DMA((got.shape[0],))],
        flops=got.size,
        moved=got.size * 2,
    )(got)


def split_sums(me, near, near_in, far, far_in):
    small = near.shape[0] // 2

    def half(x, group):
        return lax.dynamic_slice_in_dim(x, group * small, small, axis=0)

    near = near + near_in.astype(F32)
    far = far + far_in.astype(F32)
    g = me[1]
    return (
        half(near, g),
        half(near, 1 - g).astype(BF),
        half(far, g).astype(BF),
        half(far, 1 - g).astype(BF),
    )


def tokens_grad(me, mine, arrived, tokens, grad_hidden, gain):
    small = mine.shape[0]
    upstream = mine + sum(a.astype(F32) for a in arrived)
    own = lax.dynamic_slice_in_dim(tokens, me[1] * small, small, axis=0).astype(F32)
    own_grad = lax.dynamic_slice_in_dim(grad_hidden, me[1] * small, small, axis=0)
    return (own_grad + norm_backward(own, inverse_rms(own), gain, upstream)).astype(BF)


def join(me, mine, other):
    first = me[1] == 0
    return jnp.concatenate(
        [jnp.where(first, mine, other), jnp.where(first, other, mine)], axis=0
    )


def swap(x, head_bits, group_bit):
    flip = head_bits * 2 + group_bit
    return lax.ppermute(x, HG, [(i, i ^ flip) for i in range(8)])


def sequence(x, top, bottom):
    top, bottom = swap(top, 2, 0), swap(bottom, 2, 1)
    far = jnp.concatenate([top, bottom], axis=0)
    return [x, swap(x, 1, 0), far, swap(far, 1, 0)]


def exchange(tiles):
    count = lax.axis_size(ALL)
    tiles = tiles.reshape(count, -1, 128)
    return lax.all_to_all(tiles, ALL, 0, 0, tiled=True).reshape(-1, 128)


def body(
    tokens, grad_out, w_qkv, w_attn_out, gain_attn, gain_ffn, w_gate_up, w_down, ids, gates
):
    rows, width = tokens.shape
    half = width // 2
    experts = lax.axis_size("dp") * lax.axis_size("head")
    me = jnp.stack([lax.axis_index("head"), lax.axis_index("group")]).astype(jnp.int32)
    gain_attn, gain_ffn = gain_attn[None], gain_ffn[None]
    w_pair = w_gate_up.transpose(0, 1, 3, 2)
    ids_t, gates_t = ids.T, gates.T

    blocks = sequence(tokens, tokens[: rows // 2], tokens[rows // 2 :])
    tiles = send_grads(me, ids, ids_t, gates_t, grad_out, experts)
    got_grads = exchange(tiles)
    w_far = swap(w_attn_out, 2, 0)
    weights = [w_attn_out, swap(w_attn_out, 1, 0), w_far, swap(w_far, 1, 0)]

    query, key, value, chances, *mixed, normed = attention(me, blocks, gain_attn, w_qkv)
    heads = [mixed[0]] + [swap(mixed[k], k, 0) for k in range(1, 4)]
    mine, other = project(me, heads, weights)
    other = swap(other, 0, 1)
    hidden, tiles = send_hidden(me, ids, ids_t, tokens, mine, other, experts)
    in_grads, in_upstream = experts_early(got_grads, w_down)
    tiles, in_grads = lax.optimization_barrier((tiles, in_grads))
    got_hidden = exchange(tiles)
    got_hidden, hidden = lax.optimization_barrier((got_hidden, hidden))
    hidden_other = swap(hidden, 0, 1)

    tiles, in_rows, *saved = experts_forward(got_hidden, in_upstream, gain_ffn, w_pair)
    got_back = exchange(tiles)
    grad_pair, grad_down = expert_grads(in_rows, in_grads, *saved)

    upstream = combine(ids, ids_t, got_back, half)
    halves = (hidden, hidden_other, upstream, swap(upstream, 0, 1))
    grad_hidden, rounded, top, bottom, *grads = hidden_grad(
        me, grad_out, halves, gain_ffn, weights)
    grads = [grads[0]] + [swap(grads[k], k, 0) for k in range(1, 4)]
    all_grads = sequence(rounded, top, bottom)

    acts, near, far, near_out, far_out = attention_back(grads, query, key, value, chances, w_qkv)
    near_in = swap(near_out, 1, 0)
    far_in = swap(far_out, 1, 0)
    sent = weight_grads(acts, normed, mixed, all_grads, lax.axis_size("dp"))
    got = lax.all_to_all(sent, "dp", 0, 0, tiled=True)
    mine, near_other, far_mine, far_other = split_sums(me, near, near_in, far, far_in)
    arrived = (swap(near_other, 0, 1), swap(far_mine, 2, 0), swap(far_other, 2, 1))
    done = tokens_grad(me, mine, arrived, tokens, grad_hidden, gain_attn)
    done_other = swap(done, 0, 1)
    grad_tokens = join(me, done, done_other)
    grad_qkv, grad_attn_out = weight_sum(got)
    return (grad_tokens, grad_qkv, grad_attn_out, grad_pair.transpose(0, 1, 3, 2), grad_down)


def solution(mesh):
    return jax.shard_map(
        body,
        mesh=mesh,
        in_specs=(
            P(("dp", "head"), None),
            P(("dp", "head"), None),
            P(None, None, ("head", "group")),
            P(("head", "group"), None),
            P(),
            P(),
            P(("dp", "head"), None, None, "group"),
            P(("dp", "head"), "group", None),
            P(("dp", "head"), None),
            P(("dp", "head"), None),
        ),
        out_specs=(
            P(("dp", "head"), None),
            P(None, "dp", ("head", "group")),
            P(("head", "group"), "dp"),
            P(("dp", "head"), None, None, "group"),
            P(("dp", "head"), "group", None),
        ),
        check_vma=False,
    )
```

```python
import jax
import jax.numpy as jnp
from jax import lax
from jax.experimental import pallas as pl
from jax.experimental.pallas import tpu as pltpu
from jax.sharding import PartitionSpec as P


HD = 128
CAP = 5
BF = jnp.bfloat16
F32 = jnp.float32
ALL = ("group", "dp", "head")
HG = ("head", "group")
EPSILON = 1e-06
VMEM = pl.BlockSpec(memory_space=pltpu.VMEM)
SMEM = pl.BlockSpec(memory_space=pltpu.SMEM)
HBM = pl.BlockSpec(memory_space=pl.ANY)


def inverse_rms(values):
    return lax.rsqrt(jnp.mean(values * values, axis=-1, keepdims=True) + EPSILON)


def norm_backward(values, scaling, gain, upstream):
    weighted = upstream * gain
    normed = values * scaling
    return scaling * (weighted - normed * jnp.mean(weighted * normed, axis=-1, keepdims=True))


def dot(a, b, dims=((1,), (0,))):
    return lax.dot_general(a, b, (dims, ((), ())), preferred_element_type=F32)


def shaped(shape, dtype):
    return jax.ShapeDtypeStruct(shape, dtype)


def call(kernel, outs, specs, scratch=(), flops=0, moved=0, limit=None):
    return pl.pallas_call(
        kernel,
        out_shape=outs,
        in_specs=specs,
        out_specs=jax.tree.map(lambda _: VMEM, outs),
        scratch_shapes=list(scratch),
        cost_estimate=pl.CostEstimate(flops=flops, bytes_accessed=moved, transcendentals=0),
        compiler_params=pltpu.CompilerParams(vmem_limit_bytes=limit),
    )


def spread(scratch, values):
    slots, wide = values.shape
    n = wide // 128
    for c in range(n):
        scratch[pl.ds(c, slots, stride=n), :] = values[:, c * 128 : (c + 1) * 128]


def targets_of(ids, axis):
    rows = ids.shape[1]
    flat = [ids[k : k + 1, :].astype(F32) for k in range(2)]
    tall = [jnp.broadcast_to(f, (rows, rows)).T for f in flat]
    row_id = lax.broadcasted_iota(jnp.int32, (rows, rows), 0)
    col_id = lax.broadcasted_iota(jnp.int32, (rows, rows), 1)
    named, others = (flat, tall) if axis == 0 else (tall, flat)
    before = row_id < col_id if axis == 0 else col_id < row_id
    found = []
    for k in range(2):
        same = (others[0] == named[k]) | (others[1] == named[k])
        count = jnp.sum(jnp.where(same & before, 1.0, 0.0), axis=axis, keepdims=True)
        name = named[k] if axis == 0 else named[k][:, 0:1]
        found.append((name * CAP + count).astype(jnp.int32))
    return found


def pick_matrix(ids, slots):
    targets = targets_of(ids[...], 0)
    slot = lax.broadcasted_iota(jnp.int32, (slots, ids.shape[1]), 0)
    return slot == targets[0], slot == targets[1]


def attention_kernel(me, t0, t1, t2, t3, gain, w, query, key, value, chances, m0, m1, m2, m3, normed):
    rows = t0.shape[0]
    for k, t in enumerate((t0, t1, t2, t3)):
        values = t[...].astype(F32)
        normed[k * rows : (k + 1) * rows, :] = (values * inverse_rms(values) * gain[...]).astype(BF)
    weights = jnp.concatenate([w[0], w[1], w[2]], axis=1)
    proj = dot(normed[...], weights).astype(BF)
    q, k, v = proj[:, :HD], proj[:, HD : 2 * HD], proj[:, 2 * HD :]
    query[...] = q
    key[...] = k
    value[...] = v
    length = 4 * rows
    scores = dot(q, k, ((1,), (1,))) * HD ** (-0.5)
    row = lax.broadcasted_iota(jnp.int32, (length, length), 0)
    col = lax.broadcasted_iota(jnp.int32, (length, length), 1)
    row = ((row // rows) ^ me[0]) * rows + row % rows
    col = ((col // rows) ^ me[0]) * rows + col % rows
    scores = jnp.where(col <= row, scores, -1e30)
    powered = jnp.exp(scores - jnp.max(scores, axis=-1, keepdims=True))
    probs = powered / jnp.sum(powered, axis=-1, keepdims=True)
    chances[...] = probs
    mixed = dot(probs.astype(BF), v).astype(BF)
    for k, m in enumerate((m0, m1, m2, m3)):
        m[...] = mixed[k * rows : (k + 1) * rows]


def attention(me, blocks, gain, w_qkv):
    rows, width = blocks[0].shape
    length = 4 * rows
    head = shaped((length, HD), BF)
    return call(
        attention_kernel,
        (head, head, head, shaped((length, length), F32))
        + (shaped((rows, HD), BF),) * 4
        + (shaped((length, width), BF),),
        [SMEM] + [VMEM] * 6,
        flops=2 * length * (3 * width + 2 * length) * HD,
        moved=2 * length * width * 2 + 3 * width * HD * 2 + length * length * 4,
    )(me, *blocks, gain, w_qkv)


def project_kernel(me, m0, m1, m2, m3, w0, w1, w2, w3, mine, other):
    half = w0.shape[1] // 2
    total = []
    for j in range(2):
        part = None
        for m, w in ((m0, w0), (m1, w1), (m2, w2), (m3, w3)):
            term = dot(m[...], w[:, j * half : (j + 1) * half])
            part = term if part is None else part + term
        total.append(part)
    first = me[1] == 0
    mine[...] = jnp.where(first, total[0], total[1])
    other[...] = jnp.where(first, total[1], total[0]).astype(BF)


def project(me, mixed, weights):
    rows, width = mixed[0].shape[0], weights[0].shape[1]
    return call(
        project_kernel,
        (shaped((rows, width // 2), F32), shaped((rows, width // 2), BF)),
        [SMEM] + [VMEM] * 8,
        flops=8 * rows * HD * width,
        moved=8 * HD * width,
    )(me, *mixed, *weights)


def grads_kernel(me, ids, gates, grad_out, sent, scratch):
    half = grad_out.shape[1] // 2
    slots = CAP * sent.shape[0] // (2 * CAP * half // 128)
    first, second = pick_matrix(ids, slots)
    scale = jnp.sum(
        jnp.where(first, gates[0:1, :], 0.0) + jnp.where(second, gates[1:2, :], 0.0),
        axis=1,
        keepdims=True,
    )
    picker = (first | second).astype(BF)
    chosen = grad_out[:, pl.ds(pl.multiple_of(me[1] * half, half), half)]
    spread(scratch, dot(picker, chosen) * scale)
    tiles = scratch[...].astype(BF)
    count = tiles.shape[0]
    sent[:count, :] = tiles
    sent[count:, :] = tiles


def hidden_kernel(me, ids, tokens, mine, other, hidden, sent, scratch):
    half = mine.shape[1]
    slots = CAP * sent.shape[0] // (2 * CAP * half // 128)
    first, second = pick_matrix(ids, slots)
    picker = (first | second).astype(BF)
    chosen = tokens[:, pl.ds(pl.multiple_of(me[1] * half, half), half)].astype(F32)
    rows = (chosen + (mine[...] + other[...].astype(F32))).astype(BF)
    hidden[...] = rows
    spread(scratch, dot(picker, rows))
    tiles = scratch[...].astype(BF)
    count = tiles.shape[0]
    sent[:count, :] = tiles
    sent[count:, :] = tiles


def send_grads(me, ids, gates, grad_out, experts):
    rows, width = grad_out.shape
    tiles = experts * CAP * width // 2 // 128
    return call(
        grads_kernel,
        shaped((2 * tiles, 128), BF),
        [SMEM] + [VMEM] * 3,
        [pltpu.VMEM((tiles, 128), F32)],
        flops=2 * experts * CAP * rows * width // 2,
        moved=tiles * 512,
    )(me, ids, gates, grad_out)


def send_hidden(me, ids, tokens, mine, other, experts):
    rows, width = tokens.shape
    tiles = experts * CAP * width // 2 // 128
    return call(
        hidden_kernel,
        (shaped((rows, width // 2), BF), shaped((2 * tiles, 128), BF)),
        [SMEM] + [VMEM] * 4,
        [pltpu.VMEM((tiles, 128), F32)],
        flops=2 * experts * CAP * rows * width // 2,
        moved=tiles * 512,
    )(me, ids, tokens, mine, other)


def gathered(scratch, got, slots, wide):
    n = wide // 2 // 128
    tiles = slots * n
    pieces = []
    for g in range(2):
        scratch[...] = got[g * tiles : (g + 1) * tiles, :].astype(F32)
        pieces.extend(scratch[pl.ds(c, slots, stride=n), :] for c in range(n))
    return jnp.concatenate(pieces, axis=1)


def early_kernel(got_grads, w_down, in_grads, upstream, scratch, down_ref, sem):
    copy = pltpu.make_async_copy(w_down.at[0], down_ref, sem)
    copy.start()
    slots, width = in_grads.shape
    in_grads[...] = gathered(scratch, got_grads, slots, width).astype(BF)
    copy.wait()
    upstream[...] = dot(in_grads[...], down_ref[...], ((1,), (1,)))


def experts_early(got_grads, w_down):
    inner, width = w_down.shape[1:]
    tiles = got_grads.shape[0] // 2
    slots = tiles * 256 // width
    return call(
        early_kernel,
        (shaped((slots, width), BF), shaped((slots, inner), F32)),
        [VMEM, HBM],
        [pltpu.VMEM((tiles, 128), F32), pltpu.VMEM((inner, width), BF), pltpu.SemaphoreType.DMA],
        flops=2 * slots * width * inner,
        moved=2 * width * inner,
    )(got_grads, w_down)


def expert_kernel(
    got_hidden, upstream_ref, gain, w_pair, sent, in_rows, product, gate_grad, up_grad, scratch,
    pair_ref, sems
):
    copies = [
        pltpu.make_async_copy(w_pair.at[0, 0], pair_ref.at[0], sems.at[0]),
        pltpu.make_async_copy(w_pair.at[0, 1], pair_ref.at[1], sems.at[1]),
    ]
    for copy in copies:
        copy.start()
    slots, width = in_rows.shape
    values = gathered(scratch, got_hidden, slots, width)
    in_rows[...] = (values * inverse_rms(values) * gain[...]).astype(BF)
    rows = in_rows[...]
    copies[0].wait()
    gate_pre = dot(rows, pair_ref[0], ((1,), (1,)))
    copies[1].wait()
    up_pre = dot(rows, pair_ref[1], ((1,), (1,)))
    upstream = upstream_ref[...]
    sigma = 1.0 / (1.0 + jnp.exp(-gate_pre))
    active = gate_pre * sigma
    product[...] = (active * up_pre).astype(BF)
    gate_grad[...] = (upstream * up_pre * sigma * (1.0 + gate_pre * (1.0 - sigma))).astype(BF)
    up_grad[...] = (upstream * active).astype(BF)
    half = width // 2
    tiles = scratch.shape[0]
    for g in range(2):
        piece = slice(g * half, (g + 1) * half)
        returned = dot(gate_grad[...], pair_ref[0, :, piece]) + dot(
            up_grad[...], pair_ref[1, :, piece]
        )
        spread(scratch, returned)
        sent[g * tiles : (g + 1) * tiles, :] = scratch[...].astype(BF)


def experts_forward(got_hidden, upstream, gain, w_pair):
    inner, width = w_pair.shape[2:]
    tiles = got_hidden.shape[0] // 2
    slots = tiles * 256 // width
    row, unit = shaped((slots, width), BF), shaped((slots, inner), BF)
    return call(
        expert_kernel,
        (shaped((2 * tiles, 128), BF), row, unit, unit, unit),
        [VMEM] * 3 + [HBM],
        [
            pltpu.VMEM((tiles, 128), F32),
            pltpu.VMEM((2, inner, width), BF),
            pltpu.SemaphoreType.DMA((2,)),
        ],
        flops=8 * slots * width * inner,
        moved=4 * width * inner,
    )(got_hidden, upstream, gain, w_pair)


def expert_grads_kernel(in_rows, in_grads, product, gate_grad, up_grad, pair, down):
    rows = in_rows[...]
    pair[0, 0] = dot(gate_grad[...], rows, ((0,), (0,))).astype(BF)
    pair[0, 1] = dot(up_grad[...], rows, ((0,), (0,))).astype(BF)
    down[0] = dot(product[...], in_grads[...], ((0,), (0,))).astype(BF)


def expert_grads(in_rows, in_grads, product, gate_grad, up_grad):
    slots, width = in_rows.shape
    inner = product.shape[1]
    parts = 4
    row = pl.BlockSpec((slots, width // parts), lambda i: (0, i))
    unit = pl.BlockSpec((slots, inner), lambda i: (0, 0))
    return pl.pallas_call(
        expert_grads_kernel,
        out_shape=(shaped((1, 2, inner, width), BF), shaped((1, inner, width), BF)),
        grid=(parts,),
        in_specs=[row, row, unit, unit, unit],
        out_specs=(
            pl.BlockSpec((1, 2, inner, width // parts), lambda i: (0, 0, 0, i)),
            pl.BlockSpec((1, inner, width // parts), lambda i: (0, 0, i)),
        ),
        cost_estimate=pl.CostEstimate(
            flops=6 * slots * width * inner, bytes_accessed=6 * width * inner, transcendentals=0
        ),
    )(in_rows, in_grads, product, gate_grad, up_grad)


def combine_kernel(ids, got, out, scratch):
    rows, half = out.shape
    tiles = scratch.shape[0]
    n = half // 128
    slots = tiles // n
    scratch[...] = got[:tiles, :].astype(F32) + got[tiles:, :].astype(F32)
    values = jnp.concatenate(
        [scratch[pl.ds(c, slots, stride=n), :] for c in range(n)], axis=1
    ).astype(BF)
    slot = lax.broadcasted_iota(jnp.int32, (rows, slots), 1)
    targets = targets_of(ids[...], 1)
    picker = ((slot == targets[0]) | (slot == targets[1])).astype(BF)
    out[...] = dot(picker, values).astype(BF)


def combine(ids, got, half):
    rows = ids.shape[1]
    tiles = got.shape[0] // 2
    return call(
        combine_kernel,
        shaped((rows, half), BF),
        [VMEM] * 2,
        [pltpu.VMEM((tiles, 128), F32)],
        flops=2 * rows * tiles * 128,
        moved=tiles * 512,
    )(ids, got)


def hidden_grad_kernel(
    me, grad_out, hidden_mine, hidden_other, normed_mine, normed_other, gain, w0, w1, w2, w3,
    grad, rounded, p0, p1, p2, p3
):
    first = me[1] == 0

    def whole(mine, other):
        a, b = mine[...].astype(F32), other[...].astype(F32)
        return jnp.concatenate([jnp.where(first, a, b), jnp.where(first, b, a)], axis=1)

    hidden = whole(hidden_mine, hidden_other)
    upstream = whole(normed_mine, normed_other)
    value = grad_out[...].astype(F32) + norm_backward(
        hidden, inverse_rms(hidden), gain[...], upstream
    )
    grad[...] = value
    low = value.astype(BF)
    rounded[...] = low
    for p, w in ((p0, w0), (p1, w1), (p2, w2), (p3, w3)):
        p[...] = dot(low, w[...], ((1,), (1,))).astype(BF)


def hidden_grad(me, grad_out, halves, gain, weights):
    rows, width = grad_out.shape
    piece = shaped((rows, HD), BF)
    return call(
        hidden_grad_kernel,
        (shaped((rows, width), F32), shaped((rows, width), BF))
        + (piece,) * 4,
        [SMEM] + [VMEM] * 10,
        flops=8 * rows * width * HD,
        moved=8 * HD * width + 10 * rows * width,
    )(me, grad_out, *halves, gain, *weights)


def attention_back_kernel(
    g0, g1, g2, g3, query, key, value, chances, w, acts, near, far, near_out, far_out
):
    rows = g0.shape[0]
    grad = jnp.concatenate([g0[...], g1[...], g2[...], g3[...]], axis=0)
    probs = chances[...]
    grad_weights = dot(grad, value[...], ((1,), (1,)))
    total = jnp.sum(probs * grad_weights, axis=-1, keepdims=True)
    scores = (probs * (grad_weights - total) * HD ** (-0.5)).astype(BF)
    acts[:, :HD] = dot(scores, key[...]).astype(BF)
    acts[:, HD : 2 * HD] = dot(scores, query[...], ((0,), (0,))).astype(BF)
    acts[:, 2 * HD :] = dot(probs.astype(BF), grad, ((0,), (0,))).astype(BF)
    weights = jnp.concatenate([w[0], w[1], w[2]], axis=1)
    for k, out in enumerate((near, near_out, far, far_out)):
        part = dot(acts[k * rows : (k + 1) * rows, :], weights, ((1,), (1,)))
        out[...] = part.astype(out.dtype)


def attention_back(grads, query, key, value, chances, w_qkv):
    rows = grads[0].shape[0]
    width = w_qkv.shape[1]
    length = 4 * rows
    kept, sent = shaped((rows, width), F32), shaped((rows, width), BF)
    return call(
        attention_back_kernel,
        (shaped((length, 3 * HD), BF), kept, kept, sent, sent),
        [VMEM] * 9,
        flops=2 * length * (3 * width + 4 * length) * HD,
        moved=3 * width * HD * 2 + length * length * 4 + 3 * length * width,
    )(*grads, query, key, value, chances, w_qkv)


def weight_kernel(acts, normed, m0, m1, m2, m3, g0, g1, g2, g3, sent):
    pieces = sent.shape[0]
    wide = acts.shape[1]
    left = dot(acts[...], normed[...], ((0,), (0,))).astype(BF)
    grads = jnp.concatenate([g0[...], g1[...], g2[...], g3[...]], axis=0)
    mixed = jnp.concatenate([m0[...], m1[...], m2[...], m3[...]], axis=0)
    right = dot(mixed, grads, ((0,), (0,))).astype(BF)
    for j in range(pieces):
        sent[j, :wide, :] = left[:, j * 128 : (j + 1) * 128]
        sent[j, wide:, :] = right[:, j * 128 : (j + 1) * 128]


def weight_grads(acts, normed, mixed, grads, pieces):
    length, width = normed.shape
    return call(
        weight_kernel,
        shaped((pieces, 4 * HD, width // pieces), BF),
        [VMEM] * 10,
        flops=8 * length * width * HD,
        moved=4 * length * width + 8 * HD * width,
    )(acts, normed, *mixed, *grads)


def weight_sum_kernel(got, qkv, out, held, sems):
    count = got.shape[0]
    copies = [pltpu.make_async_copy(got.at[j], held.at[j], sems.at[j]) for j in range(count)]
    for copy in copies:
        copy.start()
    total = None
    for j, copy in enumerate(copies):
        copy.wait()
        term = held[j].astype(F32)
        total = term if total is None else total + term
    for i in range(3):
        qkv[i] = total[i * HD : (i + 1) * HD, :].T
    out[...] = total[3 * HD :, :]


def weight_sum(got):
    piece = got.shape[2]
    return call(
        weight_sum_kernel,
        (shaped((3, piece, HD), F32), shaped((HD, piece), F32)),
        [HBM],
        [pltpu.VMEM(got.shape, BF), pltpu.SemaphoreType.DMA((got.shape[0],))],
        flops=got.size,
        moved=got.size * 2,
        limit=65_000_000,
    )(got)


def split_sums(me, near, near_in, far, far_in):
    small = near.shape[0] // 2

    def half(x, group):
        return lax.dynamic_slice_in_dim(x, group * small, small, axis=0)

    near = near + near_in.astype(F32)
    far = far + far_in.astype(F32)
    g = me[1]
    return (
        half(near, g),
        half(near, 1 - g).astype(BF),
        half(far, g).astype(BF),
        half(far, 1 - g).astype(BF),
    )


def tokens_grad(me, mine, arrived, tokens, grad_hidden, gain):
    small = mine.shape[0]
    upstream = mine + sum(a.astype(F32) for a in arrived)
    own = lax.dynamic_slice_in_dim(tokens, me[1] * small, small, axis=0).astype(F32)
    own_grad = lax.dynamic_slice_in_dim(grad_hidden, me[1] * small, small, axis=0)
    return (own_grad + norm_backward(own, inverse_rms(own), gain, upstream)).astype(BF)


def join(me, mine, other):
    first = me[1] == 0
    return jnp.concatenate(
        [jnp.where(first, mine, other), jnp.where(first, other, mine)], axis=0
    )


def swap(x, head_bits, group_bit):
    flip = head_bits * 2 + group_bit
    return lax.ppermute(x, HG, [(i, i ^ flip) for i in range(8)])


def sequence(x):
    pairs = [(i, i ^ 4 ^ (i >> 1 & 1)) for i in range(8)]
    far = lax.ppermute(x, HG, pairs)
    core = swap(x, 1, 0)
    return [x, core, far, swap(far, 1, 0)]


def exchange(tiles):
    count = lax.axis_size(ALL)
    tiles = tiles.reshape(count, -1, 128)
    return lax.all_to_all(tiles, ALL, 0, 0, tiled=True).reshape(-1, 128)


def body(
    tokens, grad_out, w_qkv, w_attn_out, gain_attn, gain_ffn, w_gate_up, w_down, ids, gates
):
    _, width = tokens.shape
    half = width // 2
    experts = lax.axis_size("dp") * lax.axis_size("head")
    me = jnp.stack([lax.axis_index("head"), lax.axis_index("group")]).astype(jnp.int32)
    gain_attn, gain_ffn = gain_attn[None], gain_ffn[None]
    w_pair = w_gate_up.transpose(0, 1, 3, 2)
    ids, gates = ids.T, gates.T

    blocks = sequence(tokens)
    tiles = send_grads(me, ids, gates, grad_out, experts)
    got_grads = exchange(tiles)
    w_far = swap(w_attn_out, 2, 0)
    weights = [w_attn_out, swap(w_attn_out, 1, 0), w_far, swap(w_far, 1, 0)]

    query, key, value, chances, *mixed, normed = attention(me, blocks, gain_attn, w_qkv)
    heads = [mixed[0]] + [swap(mixed[k], k, 0) for k in range(1, 4)]
    mine, other = project(me, heads, weights)
    other = swap(other, 0, 1)
    hidden, tiles = send_hidden(me, ids, tokens, mine, other, experts)
    in_grads, in_upstream = experts_early(got_grads, w_down)
    tiles, in_grads = lax.optimization_barrier((tiles, in_grads))
    got_hidden = exchange(tiles)
    got_hidden, hidden = lax.optimization_barrier((got_hidden, hidden))
    hidden_other = swap(hidden, 0, 1)

    tiles, in_rows, *saved = experts_forward(got_hidden, in_upstream, gain_ffn, w_pair)
    got_back = exchange(tiles)
    grad_pair, grad_down = expert_grads(in_rows, in_grads, *saved)

    upstream = combine(ids, got_back, half)
    halves = (hidden, hidden_other, upstream, swap(upstream, 0, 1))
    grad_hidden, rounded, *grads = hidden_grad(
        me, grad_out, halves, gain_ffn, weights)
    grads = [grads[0]] + [swap(grads[k], k, 0) for k in range(1, 4)]
    all_grads = sequence(rounded)

    acts, near, far, near_out, far_out = attention_back(grads, query, key, value, chances, w_qkv)
    near_in = swap(near_out, 1, 0)
    far_in = swap(far_out, 1, 0)
    sent = weight_grads(acts, normed, mixed, all_grads, lax.axis_size("dp"))
    got = lax.all_to_all(sent, "dp", 0, 0, tiled=True)
    mine, near_other, far_mine, far_other = split_sums(me, near, near_in, far, far_in)
    arrived = (swap(near_other, 0, 1), swap(far_mine, 2, 0), swap(far_other, 2, 1))
    done = tokens_grad(me, mine, arrived, tokens, grad_hidden, gain_attn)
    done_other = swap(done, 0, 1)
    grad_tokens = join(me, done, done_other)
    grad_qkv, grad_attn_out = weight_sum(got)
    return (grad_tokens, grad_qkv, grad_attn_out, grad_pair.transpose(0, 1, 3, 2), grad_down)


def solution(mesh):
    return jax.shard_map(
        body,
        mesh=mesh,
        in_specs=(
            P(("dp", "head"), None),
            P(("dp", "head"), None),
            P(None, None, ("head", "group")),
            P(("head", "group"), None),
            P(),
            P(),
            P(("dp", "head"), None, None, "group"),
            P(("dp", "head"), "group", None),
            P(("dp", "head"), None),
            P(("dp", "head"), None),
        ),
        out_specs=(
            P(("dp", "head"), None),
            P(None, "dp", ("head", "group")),
            P(("head", "group"), "dp"),
            P(("dp", "head"), None, None, "group"),
            P(("dp", "head"), "group", None),
        ),
        check_vma=False,
    )
```

```python
import jax
import jax.numpy as jnp
from jax import lax
from jax.experimental import pallas as pl
from jax.experimental.pallas import tpu as pltpu
from jax.sharding import PartitionSpec as P


HD = 128
CAP = 5
BF = jnp.bfloat16
F32 = jnp.float32
ALL = ("head", "group", "dp")
HEADS = 4
DPS = 16
HG = ("head", "group")
EPSILON = 1e-06
LIMIT = 66_400_000
VMEM = pl.BlockSpec(memory_space=pltpu.VMEM)
SMEM = pl.BlockSpec(memory_space=pltpu.SMEM)
HBM = pl.BlockSpec(memory_space=pl.ANY)


def inverse_rms(values):
    return lax.rsqrt(jnp.mean(values * values, axis=-1, keepdims=True) + EPSILON)


def norm_backward(values, scaling, gain, upstream):
    weighted = upstream * gain
    normed = values * scaling
    return scaling * (weighted - normed * jnp.mean(weighted * normed, axis=-1, keepdims=True))


def dot(a, b, dims=((1,), (0,))):
    return lax.dot_general(a, b, (dims, ((), ())), preferred_element_type=F32)


def shaped(shape, dtype):
    return jax.ShapeDtypeStruct(shape, dtype)


def call(kernel, outs, specs, scratch=(), flops=0, moved=0, limit=None):
    return pl.pallas_call(
        kernel,
        out_shape=outs,
        in_specs=specs,
        out_specs=jax.tree.map(lambda _: VMEM, outs),
        scratch_shapes=list(scratch),
        cost_estimate=pl.CostEstimate(flops=flops, bytes_accessed=moved, transcendentals=0),
        compiler_params=pltpu.CompilerParams(vmem_limit_bytes=limit),
    )


def spread(scratch, values):
    slots, wide = values.shape
    n = wide // 128
    for c in range(n):
        scratch[pl.ds(c, slots, stride=n), :] = values[:, c * 128 : (c + 1) * 128]


def sections(tiles, group):
    part = tiles // HEADS
    return [
        (slice(h * part, (h + 1) * part), slice((2 * h + group) * part, (2 * h + group + 1) * part))
        for h in range(HEADS)
    ]


def targets_of(ids, axis):
    rows = ids.shape[1]
    ids = (ids & (HEADS - 1)) * DPS + lax.shift_right_logical(ids, HEADS.bit_length() - 1)
    flat = [ids[k : k + 1, :].astype(F32) for k in range(2)]
    tall = [jnp.broadcast_to(f, (rows, rows)).T for f in flat]
    row_id = lax.broadcasted_iota(jnp.int32, (rows, rows), 0)
    col_id = lax.broadcasted_iota(jnp.int32, (rows, rows), 1)
    named, others = (flat, tall) if axis == 0 else (tall, flat)
    before = row_id < col_id if axis == 0 else col_id < row_id
    found = []
    for k in range(2):
        same = (others[0] == named[k]) | (others[1] == named[k])
        count = jnp.sum(jnp.where(same & before, 1.0, 0.0), axis=axis, keepdims=True)
        name = named[k] if axis == 0 else named[k][:, 0:1]
        found.append((name * CAP + count).astype(jnp.int32))
    return found


def pick_matrix(ids, slots):
    targets = targets_of(ids[...], 0)
    slot = lax.broadcasted_iota(jnp.int32, (slots, ids.shape[1]), 0)
    return slot == targets[0], slot == targets[1]


def attention_kernel(me, t0, t1, t2, t3, gain, w, query, key, value, chances, m0, m1, m2, m3, normed):
    rows = t0.shape[0]
    for k, t in enumerate((t0, t1, t2, t3)):
        values = t[...].astype(F32)
        normed[k * rows : (k + 1) * rows, :] = (values * inverse_rms(values) * gain[...]).astype(BF)
    weights = jnp.concatenate([w[0], w[1], w[2]], axis=1)
    proj = dot(normed[...], weights).astype(BF)
    q, k, v = proj[:, :HD], proj[:, HD : 2 * HD], proj[:, 2 * HD :]
    query[...] = q
    key[...] = k
    value[...] = v
    length = 4 * rows
    scores = dot(q, k, ((1,), (1,))) * HD ** (-0.5)
    row = lax.broadcasted_iota(jnp.int32, (length, length), 0)
    col = lax.broadcasted_iota(jnp.int32, (length, length), 1)
    row = ((row // rows) ^ me[0]) * rows + row % rows
    col = ((col // rows) ^ me[0]) * rows + col % rows
    scores = jnp.where(col <= row, scores, -1e30)
    powered = jnp.exp(scores - jnp.max(scores, axis=-1, keepdims=True))
    probs = powered / jnp.sum(powered, axis=-1, keepdims=True)
    chances[...] = probs
    mixed = dot(probs.astype(BF), v).astype(BF)
    for k, m in enumerate((m0, m1, m2, m3)):
        m[...] = mixed[k * rows : (k + 1) * rows]


def attention(me, blocks, gain, w_qkv):
    rows, width = blocks[0].shape
    length = 4 * rows
    head = shaped((length, HD), BF)
    return call(
        attention_kernel,
        (head, head, head, shaped((length, length), F32))
        + (shaped((rows, HD), BF),) * 4
        + (shaped((length, width), BF),),
        [SMEM] + [VMEM] * 6,
        flops=2 * length * (3 * width + 2 * length) * HD,
        moved=2 * length * width * 2 + 3 * width * HD * 2 + length * length * 4,
    )(me, *blocks, gain, w_qkv)


def project_kernel(me, m0, m1, m2, m3, w0, w1, w2, w3, mine, other):
    half = w0.shape[1] // 2
    total = []
    for j in range(2):
        part = None
        for m, w in ((m0, w0), (m1, w1), (m2, w2), (m3, w3)):
            term = dot(m[...], w[:, j * half : (j + 1) * half])
            part = term if part is None else part + term
        total.append(part)
    first = me[1] == 0
    mine[...] = jnp.where(first, total[0], total[1])
    other[...] = jnp.where(first, total[1], total[0]).astype(BF)


def project(me, mixed, weights):
    rows, width = mixed[0].shape[0], weights[0].shape[1]
    return call(
        project_kernel,
        (shaped((rows, width // 2), F32), shaped((rows, width // 2), BF)),
        [SMEM] + [VMEM] * 8,
        flops=8 * rows * HD * width,
        moved=8 * HD * width,
    )(me, *mixed, *weights)


def grads_kernel(me, ids, gates, grad_out, sent, scratch):
    half = grad_out.shape[1] // 2
    slots = CAP * sent.shape[0] // (2 * CAP * half // 128)
    first, second = pick_matrix(ids, slots)
    scale = jnp.sum(
        jnp.where(first, gates[0:1, :], 0.0) + jnp.where(second, gates[1:2, :], 0.0),
        axis=1,
        keepdims=True,
    )
    picker = (first | second).astype(BF)
    chosen = grad_out[:, pl.ds(pl.multiple_of(me[1] * half, half), half)]
    spread(scratch, dot(picker, chosen) * scale)
    tiles = scratch[...].astype(BF)
    count = tiles.shape[0]
    for group in range(2):
        for one, every in sections(count, group):
            sent[every, :] = tiles[one, :]


def hidden_kernel(me, ids, tokens, mine, other, hidden, sent, scratch):
    half = mine.shape[1]
    slots = CAP * sent.shape[0] // (2 * CAP * half // 128)
    first, second = pick_matrix(ids, slots)
    picker = (first | second).astype(BF)
    chosen = tokens[:, pl.ds(pl.multiple_of(me[1] * half, half), half)].astype(F32)
    rows = (chosen + (mine[...] + other[...].astype(F32))).astype(BF)
    hidden[...] = rows
    spread(scratch, dot(picker, rows))
    tiles = scratch[...].astype(BF)
    count = tiles.shape[0]
    for group in range(2):
        for one, every in sections(count, group):
            sent[every, :] = tiles[one, :]


def send_grads(me, ids, gates, grad_out, experts):
    rows, width = grad_out.shape
    tiles = experts * CAP * width // 2 // 128
    return call(
        grads_kernel,
        shaped((2 * tiles, 128), BF),
        [SMEM] + [VMEM] * 3,
        [pltpu.VMEM((tiles, 128), F32)],
        flops=2 * experts * CAP * rows * width // 2,
        moved=tiles * 512,
    )(me, ids, gates, grad_out)


def send_hidden(me, ids, tokens, mine, other, experts):
    rows, width = tokens.shape
    tiles = experts * CAP * width // 2 // 128
    return call(
        hidden_kernel,
        (shaped((rows, width // 2), BF), shaped((2 * tiles, 128), BF)),
        [SMEM] + [VMEM] * 4,
        [pltpu.VMEM((tiles, 128), F32)],
        flops=2 * experts * CAP * rows * width // 2,
        moved=tiles * 512,
    )(me, ids, tokens, mine, other)


def gathered(scratch, got, slots, wide):
    n = wide // 2 // 128
    tiles = slots * n
    pieces = []
    for g in range(2):
        for one, every in sections(tiles, g):
            scratch[one, :] = got[every, :].astype(F32)
        pieces.extend(scratch[pl.ds(c, slots, stride=n), :] for c in range(n))
    return jnp.concatenate(pieces, axis=1)


def early_kernel(got_grads, w_down, in_grads, upstream, scratch, held, down_ref, sems):
    rows = pltpu.make_async_copy(got_grads, held, sems.at[0])
    rows.start()
    copy = pltpu.make_async_copy(w_down.at[0], down_ref, sems.at[1])
    copy.start()
    slots, width = in_grads.shape
    rows.wait()
    in_grads[...] = gathered(scratch, held, slots, width).astype(BF)
    copy.wait()
    upstream[...] = dot(in_grads[...], down_ref[...], ((1,), (1,)))


def experts_early(got_grads, w_down):
    inner, width = w_down.shape[1:]
    tiles = got_grads.shape[0] // 2
    slots = tiles * 256 // width
    return call(
        early_kernel,
        (shaped((slots, width), BF), shaped((slots, inner), F32)),
        [HBM, HBM],
        [
            pltpu.VMEM((tiles, 128), F32),
            pltpu.VMEM((2 * tiles, 128), BF),
            pltpu.VMEM((inner, width), BF),
            pltpu.SemaphoreType.DMA((2,)),
        ],
        flops=2 * slots * width * inner,
        moved=2 * width * inner,
        limit=LIMIT,
    )(got_grads, w_down)


def expert_kernel(
    got_hidden, upstream_ref, gain, w_pair, sent, in_rows, product, gate_grad, up_grad, scratch,
    pair_ref, sems
):
    copies = [
        pltpu.make_async_copy(w_pair.at[0, 0], pair_ref.at[0], sems.at[0]),
        pltpu.make_async_copy(w_pair.at[0, 1], pair_ref.at[1], sems.at[1]),
    ]
    for copy in copies:
        copy.start()
    slots, width = in_rows.shape
    values = gathered(scratch, got_hidden, slots, width)
    in_rows[...] = (values * inverse_rms(values) * gain[...]).astype(BF)
    rows = in_rows[...]
    copies[0].wait()
    gate_pre = dot(rows, pair_ref[0], ((1,), (1,)))
    copies[1].wait()
    up_pre = dot(rows, pair_ref[1], ((1,), (1,)))
    upstream = upstream_ref[...]
    sigma = 1.0 / (1.0 + jnp.exp(-gate_pre))
    active = gate_pre * sigma
    product[...] = (active * up_pre).astype(BF)
    gate_grad[...] = (upstream * up_pre * sigma * (1.0 + gate_pre * (1.0 - sigma))).astype(BF)
    up_grad[...] = (upstream * active).astype(BF)
    half = width // 2
    tiles = scratch.shape[0]
    for g in range(2):
        piece = slice(g * half, (g + 1) * half)
        returned = dot(gate_grad[...], pair_ref[0, :, piece]) + dot(
            up_grad[...], pair_ref[1, :, piece]
        )
        spread(scratch, returned)
        for one, every in sections(tiles, g):
            sent[every, :] = scratch[one, :].astype(BF)


def experts_forward(got_hidden, upstream, gain, w_pair):
    inner, width = w_pair.shape[2:]
    tiles = got_hidden.shape[0] // 2
    slots = tiles * 256 // width
    row, unit = shaped((slots, width), BF), shaped((slots, inner), BF)
    return call(
        expert_kernel,
        (shaped((2 * tiles, 128), BF), row, unit, unit, unit),
        [VMEM] * 3 + [HBM],
        [
            pltpu.VMEM((tiles, 128), F32),
            pltpu.VMEM((2, inner, width), BF),
            pltpu.SemaphoreType.DMA((2,)),
        ],
        flops=8 * slots * width * inner,
        moved=4 * width * inner,
    )(got_hidden, upstream, gain, w_pair)


def expert_grads_kernel(in_rows, in_grads, product, gate_grad, up_grad, pair, down):
    rows = in_rows[...]
    pair[0, 0] = dot(gate_grad[...], rows, ((0,), (0,))).astype(BF)
    pair[0, 1] = dot(up_grad[...], rows, ((0,), (0,))).astype(BF)
    down[0] = dot(product[...], in_grads[...], ((0,), (0,))).astype(BF)


def expert_grads(in_rows, in_grads, product, gate_grad, up_grad):
    slots, width = in_rows.shape
    inner = product.shape[1]
    parts = 4
    row = pl.BlockSpec((slots, width // parts), lambda i: (0, i))
    unit = pl.BlockSpec((slots, inner), lambda i: (0, 0))
    return pl.pallas_call(
        expert_grads_kernel,
        out_shape=(shaped((1, 2, inner, width), BF), shaped((1, inner, width), BF)),
        grid=(parts,),
        in_specs=[row, row, unit, unit, unit],
        out_specs=(
            pl.BlockSpec((1, 2, inner, width // parts), lambda i: (0, 0, 0, i)),
            pl.BlockSpec((1, inner, width // parts), lambda i: (0, 0, i)),
        ),
        cost_estimate=pl.CostEstimate(
            flops=6 * slots * width * inner, bytes_accessed=6 * width * inner, transcendentals=0
        ),
    )(in_rows, in_grads, product, gate_grad, up_grad)


def combine_kernel(ids, got, out, scratch):
    rows, half = out.shape
    tiles = scratch.shape[0]
    n = half // 128
    slots = tiles // n
    for (one, first), (_, second) in zip(sections(tiles, 0), sections(tiles, 1)):
        scratch[one, :] = got[first, :].astype(F32) + got[second, :].astype(F32)
    values = jnp.concatenate(
        [scratch[pl.ds(c, slots, stride=n), :] for c in range(n)], axis=1
    ).astype(BF)
    slot = lax.broadcasted_iota(jnp.int32, (rows, slots), 1)
    targets = targets_of(ids[...], 1)
    picker = ((slot == targets[0]) | (slot == targets[1])).astype(BF)
    out[...] = dot(picker, values).astype(BF)


def combine(ids, got, half):
    rows = ids.shape[1]
    tiles = got.shape[0] // 2
    return call(
        combine_kernel,
        shaped((rows, half), BF),
        [VMEM] * 2,
        [pltpu.VMEM((tiles, 128), F32)],
        flops=2 * rows * tiles * 128,
        moved=tiles * 512,
    )(ids, got)


def hidden_grad_kernel(
    me, grad_out, hidden_mine, hidden_other, normed_mine, normed_other, gain, w0, w1, w2, w3,
    grad, rounded, p0, p1, p2, p3
):
    first = me[1] == 0

    def whole(mine, other):
        a, b = mine[...].astype(F32), other[...].astype(F32)
        return jnp.concatenate([jnp.where(first, a, b), jnp.where(first, b, a)], axis=1)

    hidden = whole(hidden_mine, hidden_other)
    upstream = whole(normed_mine, normed_other)
    value = grad_out[...].astype(F32) + norm_backward(
        hidden, inverse_rms(hidden), gain[...], upstream
    )
    grad[...] = value
    low = value.astype(BF)
    rounded[...] = low
    for p, w in ((p0, w0), (p1, w1), (p2, w2), (p3, w3)):
        p[...] = dot(low, w[...], ((1,), (1,))).astype(BF)


def hidden_grad(me, grad_out, halves, gain, weights):
    rows, width = grad_out.shape
    piece = shaped((rows, HD), BF)
    return call(
        hidden_grad_kernel,
        (shaped((rows, width), F32), shaped((rows, width), BF))
        + (piece,) * 4,
        [SMEM] + [VMEM] * 10,
        flops=8 * rows * width * HD,
        moved=8 * HD * width + 10 * rows * width,
    )(me, grad_out, *halves, gain, *weights)


def attention_back_kernel(
    g0, g1, g2, g3, query, key, value, chances, w, acts, near, far, near_out, far_out
):
    rows = g0.shape[0]
    grad = jnp.concatenate([g0[...], g1[...], g2[...], g3[...]], axis=0)
    probs = chances[...]
    grad_weights = dot(grad, value[...], ((1,), (1,)))
    total = jnp.sum(probs * grad_weights, axis=-1, keepdims=True)
    scores = (probs * (grad_weights - total) * HD ** (-0.5)).astype(BF)
    acts[:, :HD] = dot(scores, key[...]).astype(BF)
    acts[:, HD : 2 * HD] = dot(scores, query[...], ((0,), (0,))).astype(BF)
    acts[:, 2 * HD :] = dot(probs.astype(BF), grad, ((0,), (0,))).astype(BF)
    weights = jnp.concatenate([w[0], w[1], w[2]], axis=1)
    for k, out in enumerate((near, near_out, far, far_out)):
        part = dot(acts[k * rows : (k + 1) * rows, :], weights, ((1,), (1,)))
        out[...] = part.astype(out.dtype)


def attention_back(grads, query, key, value, chances, w_qkv):
    rows = grads[0].shape[0]
    width = w_qkv.shape[1]
    length = 4 * rows
    kept, sent = shaped((rows, width), F32), shaped((rows, width), BF)
    return call(
        attention_back_kernel,
        (shaped((length, 3 * HD), BF), kept, kept, sent, sent),
        [VMEM] * 9,
        flops=2 * length * (3 * width + 4 * length) * HD,
        moved=3 * width * HD * 2 + length * length * 4 + 3 * length * width,
    )(*grads, query, key, value, chances, w_qkv)


def weight_kernel(acts, normed, m0, m1, m2, m3, g0, g1, g2, g3, sent):
    pieces = sent.shape[0]
    wide = acts.shape[1]
    left = dot(acts[...], normed[...], ((0,), (0,))).astype(BF)
    grads = jnp.concatenate([g0[...], g1[...], g2[...], g3[...]], axis=0)
    mixed = jnp.concatenate([m0[...], m1[...], m2[...], m3[...]], axis=0)
    right = dot(mixed, grads, ((0,), (0,))).astype(BF)
    for j in range(pieces):
        sent[j, :wide, :] = left[:, j * 128 : (j + 1) * 128]
        sent[j, wide:, :] = right[:, j * 128 : (j + 1) * 128]


def weight_grads(acts, normed, mixed, grads, pieces):
    length, width = normed.shape
    return call(
        weight_kernel,
        shaped((pieces, 4 * HD, width // pieces), BF),
        [VMEM] * 10,
        flops=8 * length * width * HD,
        moved=4 * length * width + 8 * HD * width,
    )(acts, normed, *mixed, *grads)


def weight_sum_kernel(got, qkv, out, held, sems):
    count = got.shape[0]
    copies = [pltpu.make_async_copy(got.at[j], held.at[j], sems.at[j]) for j in range(count)]
    for copy in copies:
        copy.start()
    total = None
    for j, copy in enumerate(copies):
        copy.wait()
        term = held[j].astype(F32)
        total = term if total is None else total + term
    for i in range(3):
        qkv[i] = total[i * HD : (i + 1) * HD, :].T
    out[...] = total[3 * HD :, :]


def weight_sum(got):
    piece = got.shape[2]
    return call(
        weight_sum_kernel,
        (shaped((3, piece, HD), F32), shaped((HD, piece), F32)),
        [HBM],
        [pltpu.VMEM(got.shape, BF), pltpu.SemaphoreType.DMA((got.shape[0],))],
        flops=got.size,
        moved=got.size * 2,
        limit=LIMIT,
    )(got)


def split_sums(me, near, near_in, far, far_in):
    small = near.shape[0] // 2

    def half(x, group):
        return lax.dynamic_slice_in_dim(x, group * small, small, axis=0)

    near = near + near_in.astype(F32)
    far = far + far_in.astype(F32)
    g = me[1]
    return (
        half(near, g),
        half(near, 1 - g).astype(BF),
        half(far, g).astype(BF),
        half(far, 1 - g).astype(BF),
    )


def tokens_grad(me, mine, arrived, tokens, grad_hidden, gain):
    small = mine.shape[0]
    upstream = mine + sum(a.astype(F32) for a in arrived)
    own = lax.dynamic_slice_in_dim(tokens, me[1] * small, small, axis=0).astype(F32)
    own_grad = lax.dynamic_slice_in_dim(grad_hidden, me[1] * small, small, axis=0)
    return (own_grad + norm_backward(own, inverse_rms(own), gain, upstream)).astype(BF)


def join(me, mine, other):
    first = me[1] == 0
    return jnp.concatenate(
        [jnp.where(first, mine, other), jnp.where(first, other, mine)], axis=0
    )


def swap(x, head_bits, group_bit):
    flip = head_bits * 2 + group_bit
    return lax.ppermute(x, HG, [(i, i ^ flip) for i in range(8)])


def sequence(x):
    pairs = [(i, i ^ 4 ^ (i >> 1 & 1)) for i in range(8)]
    far = lax.ppermute(x, HG, pairs)
    core = swap(x, 1, 0)
    return [x, core, far, swap(far, 1, 0)]


def exchange(tiles):
    count = lax.axis_size(ALL)
    tiles = tiles.reshape(count, -1, 128)
    return lax.all_to_all(tiles, ALL, 0, 0, tiled=True).reshape(-1, 128)


def body(
    tokens, grad_out, w_qkv, w_attn_out, gain_attn, gain_ffn, w_gate_up, w_down, ids, gates
):
    _, width = tokens.shape
    half = width // 2
    experts = lax.axis_size("dp") * lax.axis_size("head")
    me = jnp.stack([lax.axis_index("head"), lax.axis_index("group")]).astype(jnp.int32)
    gain_attn, gain_ffn = gain_attn[None], gain_ffn[None]
    w_pair = w_gate_up.transpose(0, 1, 3, 2)
    ids, gates = ids.T, gates.T

    blocks = sequence(tokens)
    tiles = send_grads(me, ids, gates, grad_out, experts)
    got_grads = exchange(tiles)
    w_far = swap(w_attn_out, 2, 0)
    weights = [w_attn_out, swap(w_attn_out, 1, 0), w_far, swap(w_far, 1, 0)]

    query, key, value, chances, *mixed, normed = attention(me, blocks, gain_attn, w_qkv)
    heads = [mixed[0]] + [swap(mixed[k], k, 0) for k in range(1, 4)]
    mine, other = project(me, heads, weights)
    other = swap(other, 0, 1)
    hidden, tiles = send_hidden(me, ids, tokens, mine, other, experts)
    in_grads, in_upstream = experts_early(got_grads, w_down)
    tiles, in_grads = lax.optimization_barrier((tiles, in_grads))
    got_hidden = exchange(tiles)
    got_hidden, hidden = lax.optimization_barrier((got_hidden, hidden))
    hidden_other = swap(hidden, 0, 1)

    tiles, in_rows, *saved = experts_forward(got_hidden, in_upstream, gain_ffn, w_pair)
    got_back = exchange(tiles)
    grad_pair, grad_down = expert_grads(in_rows, in_grads, *saved)

    upstream = combine(ids, got_back, half)
    halves = (hidden, hidden_other, upstream, swap(upstream, 0, 1))
    grad_hidden, rounded, *grads = hidden_grad(
        me, grad_out, halves, gain_ffn, weights)
    grads = [grads[0]] + [swap(grads[k], k, 0) for k in range(1, 4)]
    all_grads = sequence(rounded)

    acts, near, far, near_out, far_out = attention_back(grads, query, key, value, chances, w_qkv)
    near_in = swap(near_out, 1, 0)
    far_in = swap(far_out, 1, 0)
    sent = weight_grads(acts, normed, mixed, all_grads, lax.axis_size("dp"))
    got = lax.all_to_all(sent, "dp", 0, 0, tiled=True)
    mine, near_other, far_mine, far_other = split_sums(me, near, near_in, far, far_in)
    arrived = (swap(near_other, 0, 1), swap(far_mine, 2, 0), swap(far_other, 2, 1))
    done = tokens_grad(me, mine, arrived, tokens, grad_hidden, gain_attn)
    done_other = swap(done, 0, 1)
    grad_tokens = join(me, done, done_other)
    grad_qkv, grad_attn_out = weight_sum(got)
    return (grad_tokens, grad_qkv, grad_attn_out, grad_pair.transpose(0, 1, 3, 2), grad_down)


def solution(mesh):
    return jax.shard_map(
        body,
        mesh=mesh,
        in_specs=(
            P(("dp", "head"), None),
            P(("dp", "head"), None),
            P(None, None, ("head", "group")),
            P(("head", "group"), None),
            P(),
            P(),
            P(("dp", "head"), None, None, "group"),
            P(("dp", "head"), "group", None),
            P(("dp", "head"), None),
            P(("dp", "head"), None),
        ),
        out_specs=(
            P(("dp", "head"), None),
            P(None, "dp", ("head", "group")),
            P(("head", "group"), "dp"),
            P(("dp", "head"), None, None, "group"),
            P(("dp", "head"), "group", None),
        ),
        check_vma=False,
    )
```

```python
import jax
import jax.numpy as jnp
from jax import lax
from jax.experimental import pallas as pl
from jax.experimental.pallas import tpu as pltpu
from jax.sharding import PartitionSpec as P


HD = 128
CAP = 5
BF = jnp.bfloat16
F32 = jnp.float32
ALL = ("head", "group", "dp")
HEADS = 4
DPS = 16
HG = ("head", "group")
EPSILON = 1e-06
LIMIT = 66_400_000
VMEM = pl.BlockSpec(memory_space=pltpu.VMEM)
SMEM = pl.BlockSpec(memory_space=pltpu.SMEM)
HBM = pl.BlockSpec(memory_space=pl.ANY)


def inverse_rms(values):
    return lax.rsqrt(jnp.mean(values * values, axis=-1, keepdims=True) + EPSILON)


def norm_backward(values, scaling, gain, upstream):
    weighted = upstream * gain
    normed = values * scaling
    return scaling * (weighted - normed * jnp.mean(weighted * normed, axis=-1, keepdims=True))


def dot(a, b, dims=((1,), (0,))):
    return lax.dot_general(a, b, (dims, ((), ())), preferred_element_type=F32)


def shaped(shape, dtype):
    return jax.ShapeDtypeStruct(shape, dtype)


def call(kernel, outs, specs, scratch=(), flops=0, moved=0, limit=None):
    return pl.pallas_call(
        kernel,
        out_shape=outs,
        in_specs=specs,
        out_specs=jax.tree.map(lambda _: VMEM, outs),
        scratch_shapes=list(scratch),
        cost_estimate=pl.CostEstimate(flops=flops, bytes_accessed=moved, transcendentals=0),
        compiler_params=pltpu.CompilerParams(vmem_limit_bytes=limit),
    )


def spread(scratch, values):
    slots, wide = values.shape
    n = wide // 128
    for c in range(n):
        scratch[pl.ds(c, slots, stride=n), :] = values[:, c * 128 : (c + 1) * 128]


def sections(tiles, group):
    part = tiles // HEADS
    return [
        (slice(h * part, (h + 1) * part), slice((2 * h + group) * part, (2 * h + group + 1) * part))
        for h in range(HEADS)
    ]


def targets_of(ids, axis):
    rows = ids.shape[1]
    ids = (ids & (HEADS - 1)) * DPS + lax.shift_right_logical(ids, HEADS.bit_length() - 1)
    flat = [ids[k : k + 1, :].astype(F32) for k in range(2)]
    tall = [jnp.broadcast_to(f, (rows, rows)).T for f in flat]
    row_id = lax.broadcasted_iota(jnp.int32, (rows, rows), 0)
    col_id = lax.broadcasted_iota(jnp.int32, (rows, rows), 1)
    named, others = (flat, tall) if axis == 0 else (tall, flat)
    before = row_id < col_id if axis == 0 else col_id < row_id
    found = []
    for k in range(2):
        same = (others[0] == named[k]) | (others[1] == named[k])
        count = jnp.sum(jnp.where(same & before, 1.0, 0.0), axis=axis, keepdims=True)
        name = named[k] if axis == 0 else named[k][:, 0:1]
        found.append((name * CAP + count).astype(jnp.int32))
    return found


def pick_matrix(ids, slots):
    targets = targets_of(ids[...], 0)
    slot = lax.broadcasted_iota(jnp.int32, (slots, ids.shape[1]), 0)
    return slot == targets[0], slot == targets[1]


def attention_kernel(me, t0, t1, t2, t3, gain, w, query, key, value, chances, m0, m1, m2, m3, normed):
    rows = t0.shape[0]
    for k, t in enumerate((t0, t1, t2, t3)):
        values = t[...].astype(F32)
        normed[k * rows : (k + 1) * rows, :] = (values * inverse_rms(values) * gain[...]).astype(BF)
    weights = jnp.concatenate([w[0], w[1], w[2]], axis=1)
    proj = dot(normed[...], weights).astype(BF)
    q, k, v = proj[:, :HD], proj[:, HD : 2 * HD], proj[:, 2 * HD :]
    query[...] = q
    key[...] = k
    value[...] = v
    length = 4 * rows
    scores = dot(q, k, ((1,), (1,))) * HD ** (-0.5)
    row = lax.broadcasted_iota(jnp.int32, (length, length), 0)
    col = lax.broadcasted_iota(jnp.int32, (length, length), 1)
    row = ((row // rows) ^ me[0]) * rows + row % rows
    col = ((col // rows) ^ me[0]) * rows + col % rows
    scores = jnp.where(col <= row, scores, -1e30)
    powered = jnp.exp(scores - jnp.max(scores, axis=-1, keepdims=True))
    probs = powered / jnp.sum(powered, axis=-1, keepdims=True)
    chances[...] = probs
    mixed = dot(probs.astype(BF), v).astype(BF)
    for k, m in enumerate((m0, m1, m2, m3)):
        m[...] = mixed[k * rows : (k + 1) * rows]


def attention(me, blocks, gain, w_qkv):
    rows, width = blocks[0].shape
    length = 4 * rows
    head = shaped((length, HD), BF)
    return call(
        attention_kernel,
        (head, head, head, shaped((length, length), F32))
        + (shaped((rows, HD), BF),) * 4
        + (shaped((length, width), BF),),
        [SMEM] + [VMEM] * 6,
        flops=2 * length * (3 * width + 2 * length) * HD,
        moved=2 * length * width * 2 + 3 * width * HD * 2 + length * length * 4,
    )(me, *blocks, gain, w_qkv)


def project_kernel(me, m0, m1, m2, m3, w0, w1, w2, w3, mine, other):
    half = w0.shape[1] // 2
    total = []
    for j in range(2):
        part = None
        for m, w in ((m0, w0), (m1, w1), (m2, w2), (m3, w3)):
            term = dot(m[...], w[:, j * half : (j + 1) * half])
            part = term if part is None else part + term
        total.append(part)
    first = me[1] == 0
    mine[...] = jnp.where(first, total[0], total[1])
    other[...] = jnp.where(first, total[1], total[0]).astype(BF)


def project(me, mixed, weights):
    rows, width = mixed[0].shape[0], weights[0].shape[1]
    return call(
        project_kernel,
        (shaped((rows, width // 2), F32), shaped((rows, width // 2), BF)),
        [SMEM] + [VMEM] * 8,
        flops=8 * rows * HD * width,
        moved=8 * HD * width,
    )(me, *mixed, *weights)


def grads_kernel(me, ids, gates, grad_out, sent, scratch):
    half = grad_out.shape[1] // 2
    slots = CAP * sent.shape[0] // (2 * CAP * half // 128)
    first, second = pick_matrix(ids, slots)
    scale = jnp.sum(
        jnp.where(first, gates[0:1, :], 0.0) + jnp.where(second, gates[1:2, :], 0.0),
        axis=1,
        keepdims=True,
    )
    picker = (first | second).astype(BF)
    chosen = grad_out[:, pl.ds(pl.multiple_of(me[1] * half, half), half)]
    spread(scratch, dot(picker, chosen) * scale)
    tiles = scratch[...].astype(BF)
    count = tiles.shape[0]
    for group in range(2):
        for one, every in sections(count, group):
            sent[every, :] = tiles[one, :]


def hidden_kernel(me, ids, tokens, mine, other, hidden, sent, scratch):
    half = mine.shape[1]
    slots = CAP * sent.shape[0] // (2 * CAP * half // 128)
    first, second = pick_matrix(ids, slots)
    picker = (first | second).astype(BF)
    chosen = tokens[:, pl.ds(pl.multiple_of(me[1] * half, half), half)].astype(F32)
    rows = (chosen + (mine[...] + other[...].astype(F32))).astype(BF)
    hidden[...] = rows
    spread(scratch, dot(picker, rows))
    tiles = scratch[...].astype(BF)
    count = tiles.shape[0]
    for group in range(2):
        for one, every in sections(count, group):
            sent[every, :] = tiles[one, :]


def send_grads(me, ids, gates, grad_out, experts):
    rows, width = grad_out.shape
    tiles = experts * CAP * width // 2 // 128
    return call(
        grads_kernel,
        shaped((2 * tiles, 128), BF),
        [SMEM] + [VMEM] * 3,
        [pltpu.VMEM((tiles, 128), F32)],
        flops=2 * experts * CAP * rows * width // 2,
        moved=tiles * 512,
    )(me, ids, gates, grad_out)


def send_hidden(me, ids, tokens, mine, other, experts):
    rows, width = tokens.shape
    tiles = experts * CAP * width // 2 // 128
    return call(
        hidden_kernel,
        (shaped((rows, width // 2), BF), shaped((2 * tiles, 128), BF)),
        [SMEM] + [VMEM] * 4,
        [pltpu.VMEM((tiles, 128), F32)],
        flops=2 * experts * CAP * rows * width // 2,
        moved=tiles * 512,
    )(me, ids, tokens, mine, other)


def gathered(scratch, got, slots, wide):
    n = wide // 2 // 128
    tiles = slots * n
    pieces = []
    for g in range(2):
        for one, every in sections(tiles, g):
            scratch[one, :] = got[every, :].astype(F32)
        pieces.extend(scratch[pl.ds(c, slots, stride=n), :] for c in range(n))
    return jnp.concatenate(pieces, axis=1)


def early_kernel(got_grads, w_down, in_grads, upstream, scratch, held, down_ref, sems):
    rows = pltpu.make_async_copy(got_grads, held, sems.at[0])
    rows.start()
    copy = pltpu.make_async_copy(w_down.at[0], down_ref, sems.at[1])
    copy.start()
    slots, width = in_grads.shape
    rows.wait()
    in_grads[...] = gathered(scratch, held, slots, width).astype(BF)
    copy.wait()
    upstream[...] = dot(in_grads[...], down_ref[...], ((1,), (1,)))


def experts_early(got_grads, w_down):
    inner, width = w_down.shape[1:]
    tiles = got_grads.shape[0] // 2
    slots = tiles * 256 // width
    return call(
        early_kernel,
        (shaped((slots, width), BF), shaped((slots, inner), F32)),
        [HBM, HBM],
        [
            pltpu.VMEM((tiles, 128), F32),
            pltpu.VMEM((2 * tiles, 128), BF),
            pltpu.VMEM((inner, width), BF),
            pltpu.SemaphoreType.DMA((2,)),
        ],
        flops=2 * slots * width * inner,
        moved=2 * width * inner,
        limit=LIMIT,
    )(got_grads, w_down)


def expert_kernel(
    got_hidden, upstream_ref, gain, w_pair, sent, in_rows, product, gate_grad, up_grad, scratch,
    pair_ref, sems
):
    copies = [
        pltpu.make_async_copy(w_pair.at[0, 0], pair_ref.at[0], sems.at[0]),
        pltpu.make_async_copy(w_pair.at[0, 1], pair_ref.at[1], sems.at[1]),
    ]
    for copy in copies:
        copy.start()
    slots, width = in_rows.shape
    values = gathered(scratch, got_hidden, slots, width)
    in_rows[...] = (values * inverse_rms(values) * gain[...]).astype(BF)
    rows = in_rows[...]
    copies[0].wait()
    gate_pre = dot(rows, pair_ref[0], ((1,), (1,)))
    copies[1].wait()
    up_pre = dot(rows, pair_ref[1], ((1,), (1,)))
    upstream = upstream_ref[...]
    sigma = 1.0 / (1.0 + jnp.exp(-gate_pre))
    active = gate_pre * sigma
    product[...] = (active * up_pre).astype(BF)
    gate_grad[...] = (upstream * up_pre * sigma * (1.0 + gate_pre * (1.0 - sigma))).astype(BF)
    up_grad[...] = (upstream * active).astype(BF)
    half = width // 2
    tiles = scratch.shape[0]
    for g in range(2):
        piece = slice(g * half, (g + 1) * half)
        returned = dot(gate_grad[...], pair_ref[0, :, piece]) + dot(
            up_grad[...], pair_ref[1, :, piece]
        )
        spread(scratch, returned)
        for one, every in sections(tiles, g):
            sent[every, :] = scratch[one, :].astype(BF)


def experts_forward(got_hidden, upstream, gain, w_pair):
    inner, width = w_pair.shape[2:]
    tiles = got_hidden.shape[0] // 2
    slots = tiles * 256 // width
    row, unit = shaped((slots, width), BF), shaped((slots, inner), BF)
    return call(
        expert_kernel,
        (shaped((2 * tiles, 128), BF), row, unit, unit, unit),
        [VMEM] * 3 + [HBM],
        [
            pltpu.VMEM((tiles, 128), F32),
            pltpu.VMEM((2, inner, width), BF),
            pltpu.SemaphoreType.DMA((2,)),
        ],
        flops=8 * slots * width * inner,
        moved=4 * width * inner,
    )(got_hidden, upstream, gain, w_pair)


def expert_grads_kernel(in_rows, in_grads, product, gate_grad, up_grad, pair, down):
    rows = in_rows[...]
    pair[0, 0] = dot(gate_grad[...], rows, ((0,), (0,))).astype(BF)
    pair[0, 1] = dot(up_grad[...], rows, ((0,), (0,))).astype(BF)
    down[0] = dot(product[...], in_grads[...], ((0,), (0,))).astype(BF)


def expert_grads(in_rows, in_grads, product, gate_grad, up_grad):
    slots, width = in_rows.shape
    inner = product.shape[1]
    parts = 4
    row = pl.BlockSpec((slots, width // parts), lambda i: (0, i))
    unit = pl.BlockSpec((slots, inner), lambda i: (0, 0))
    return pl.pallas_call(
        expert_grads_kernel,
        out_shape=(shaped((1, 2, inner, width), BF), shaped((1, inner, width), BF)),
        grid=(parts,),
        in_specs=[row, row, unit, unit, unit],
        out_specs=(
            pl.BlockSpec((1, 2, inner, width // parts), lambda i: (0, 0, 0, i)),
            pl.BlockSpec((1, inner, width // parts), lambda i: (0, 0, i)),
        ),
        cost_estimate=pl.CostEstimate(
            flops=6 * slots * width * inner, bytes_accessed=6 * width * inner, transcendentals=0
        ),
    )(in_rows, in_grads, product, gate_grad, up_grad)


def combine_kernel(ids, got, out, scratch):
    rows, half = out.shape
    tiles = scratch.shape[0]
    n = half // 128
    slots = tiles // n
    for (one, first), (_, second) in zip(sections(tiles, 0), sections(tiles, 1)):
        scratch[one, :] = got[first, :].astype(F32) + got[second, :].astype(F32)
    values = jnp.concatenate(
        [scratch[pl.ds(c, slots, stride=n), :] for c in range(n)], axis=1
    ).astype(BF)
    slot = lax.broadcasted_iota(jnp.int32, (rows, slots), 1)
    targets = targets_of(ids[...], 1)
    picker = ((slot == targets[0]) | (slot == targets[1])).astype(BF)
    out[...] = dot(picker, values).astype(BF)


def combine(ids, got, half):
    rows = ids.shape[1]
    tiles = got.shape[0] // 2
    return call(
        combine_kernel,
        shaped((rows, half), BF),
        [VMEM] * 2,
        [pltpu.VMEM((tiles, 128), F32)],
        flops=2 * rows * tiles * 128,
        moved=tiles * 512,
    )(ids, got)


def hidden_grad_kernel(
    me, grad_out, hidden_mine, hidden_other, normed_mine, normed_other, gain, w0, w1, w2, w3,
    grad, rounded, p0, p1, p2, p3
):
    first = me[1] == 0

    def whole(mine, other):
        a, b = mine[...].astype(F32), other[...].astype(F32)
        return jnp.concatenate([jnp.where(first, a, b), jnp.where(first, b, a)], axis=1)

    hidden = whole(hidden_mine, hidden_other)
    upstream = whole(normed_mine, normed_other)
    value = grad_out[...].astype(F32) + norm_backward(
        hidden, inverse_rms(hidden), gain[...], upstream
    )
    grad[...] = value
    low = value.astype(BF)
    rounded[...] = low
    for p, w in ((p0, w0), (p1, w1), (p2, w2), (p3, w3)):
        p[...] = dot(low, w[...], ((1,), (1,))).astype(BF)


def hidden_grad(me, grad_out, halves, gain, weights):
    rows, width = grad_out.shape
    piece = shaped((rows, HD), BF)
    return call(
        hidden_grad_kernel,
        (shaped((rows, width), F32), shaped((rows, width), BF))
        + (piece,) * 4,
        [SMEM] + [VMEM] * 10,
        flops=8 * rows * width * HD,
        moved=8 * HD * width + 10 * rows * width,
    )(me, grad_out, *halves, gain, *weights)


def attention_back_kernel(
    g0, g1, g2, g3, query, key, value, chances, w, acts, near, far, near_out, far_out
):
    rows = g0.shape[0]
    grad = jnp.concatenate([g0[...], g1[...], g2[...], g3[...]], axis=0)
    probs = chances[...]
    grad_weights = dot(grad, value[...], ((1,), (1,)))
    total = jnp.sum(probs * grad_weights, axis=-1, keepdims=True)
    scores = (probs * (grad_weights - total) * HD ** (-0.5)).astype(BF)
    acts[:, :HD] = dot(scores, key[...]).astype(BF)
    acts[:, HD : 2 * HD] = dot(scores, query[...], ((0,), (0,))).astype(BF)
    acts[:, 2 * HD :] = dot(probs.astype(BF), grad, ((0,), (0,))).astype(BF)
    weights = jnp.concatenate([w[0], w[1], w[2]], axis=1)
    for k, out in enumerate((near, near_out, far, far_out)):
        part = dot(acts[k * rows : (k + 1) * rows, :], weights, ((1,), (1,)))
        out[...] = part.astype(out.dtype)


def attention_back(grads, query, key, value, chances, w_qkv):
    rows = grads[0].shape[0]
    width = w_qkv.shape[1]
    length = 4 * rows
    kept, sent = shaped((rows, width), F32), shaped((rows, width), BF)
    return call(
        attention_back_kernel,
        (shaped((length, 3 * HD), BF), kept, kept, sent, sent),
        [VMEM] * 9,
        flops=2 * length * (3 * width + 4 * length) * HD,
        moved=3 * width * HD * 2 + length * length * 4 + 3 * length * width,
    )(*grads, query, key, value, chances, w_qkv)


def weight_kernel(acts, normed, m0, m1, m2, m3, g0, g1, g2, g3, sent):
    pieces = sent.shape[0]
    wide = acts.shape[1]
    left = dot(acts[...], normed[...], ((0,), (0,))).astype(BF)
    grads = jnp.concatenate([g0[...], g1[...], g2[...], g3[...]], axis=0)
    mixed = jnp.concatenate([m0[...], m1[...], m2[...], m3[...]], axis=0)
    right = dot(mixed, grads, ((0,), (0,))).astype(BF)
    for j in range(pieces):
        sent[j, :wide, :] = left[:, j * 128 : (j + 1) * 128]
        sent[j, wide:, :] = right[:, j * 128 : (j + 1) * 128]


def weight_grads(acts, normed, mixed, grads, pieces):
    length, width = normed.shape
    return call(
        weight_kernel,
        shaped((pieces, 4 * HD, width // pieces), BF),
        [VMEM] * 10,
        flops=8 * length * width * HD,
        moved=4 * length * width + 8 * HD * width,
    )(acts, normed, *mixed, *grads)


def weight_sum_kernel(got, qkv, out, held, sems):
    count = got.shape[0]
    copies = [pltpu.make_async_copy(got.at[j], held.at[j], sems.at[j]) for j in range(count)]
    for copy in copies:
        copy.start()
    total = None
    for j, copy in enumerate(copies):
        copy.wait()
        term = held[j].astype(F32)
        total = term if total is None else total + term
    for i in range(3):
        qkv[i] = total[i * HD : (i + 1) * HD, :].T
    out[...] = total[3 * HD :, :]


def weight_sum(got):
    piece = got.shape[2]
    return call(
        weight_sum_kernel,
        (shaped((3, piece, HD), F32), shaped((HD, piece), F32)),
        [HBM],
        [pltpu.VMEM(got.shape, BF), pltpu.SemaphoreType.DMA((got.shape[0],))],
        flops=got.size,
        moved=got.size * 2,
        limit=LIMIT,
    )(got)


def split_sums(me, near, near_in, far, far_in):
    small = near.shape[0] // 2

    def half(x, group):
        return lax.dynamic_slice_in_dim(x, group * small, small, axis=0)

    near = near + near_in.astype(F32)
    far = far + far_in.astype(F32)
    g = me[1]
    return (
        half(near, g),
        half(near, 1 - g).astype(BF),
        half(far, g).astype(BF),
        half(far, 1 - g).astype(BF),
    )


def tokens_grad(me, mine, arrived, tokens, grad_hidden, gain):
    small = mine.shape[0]
    upstream = mine + sum(a.astype(F32) for a in arrived)
    own = lax.dynamic_slice_in_dim(tokens, me[1] * small, small, axis=0).astype(F32)
    own_grad = lax.dynamic_slice_in_dim(grad_hidden, me[1] * small, small, axis=0)
    return (own_grad + norm_backward(own, inverse_rms(own), gain, upstream)).astype(BF)


def join(me, mine, other):
    first = me[1] == 0
    return jnp.concatenate(
        [jnp.where(first, mine, other), jnp.where(first, other, mine)], axis=0
    )


def swap(x, head_bits, group_bit):
    flip = head_bits * 2 + group_bit
    return lax.ppermute(x, HG, [(i, i ^ flip) for i in range(8)])


def sequence(x, split):
    pairs = [(i, i ^ 4 ^ (i >> 1 & 1 if split else 1)) for i in range(8)]
    far = lax.ppermute(x, HG, pairs)
    core = swap(x, 1, 0)
    return [x, core, far, swap(far, 1, 0)]


def exchange(tiles):
    count = lax.axis_size(ALL)
    tiles = tiles.reshape(count, -1, 128)
    return lax.all_to_all(tiles, ALL, 0, 0, tiled=True).reshape(-1, 128)


def body(
    tokens, grad_out, w_qkv, w_attn_out, gain_attn, gain_ffn, w_gate_up, w_down, ids, gates
):
    _, width = tokens.shape
    half = width // 2
    experts = lax.axis_size("dp") * lax.axis_size("head")
    me = jnp.stack([lax.axis_index("head"), lax.axis_index("group")]).astype(jnp.int32)
    gain_attn, gain_ffn = gain_attn[None], gain_ffn[None]
    w_pair = w_gate_up.transpose(0, 1, 3, 2)
    ids, gates = ids.T, gates.T

    blocks = sequence(tokens, False)
    tiles = send_grads(me, ids, gates, grad_out, experts)
    got_grads = exchange(tiles)
    w_far = swap(w_attn_out, 2, 0)
    weights = [w_attn_out, swap(w_attn_out, 1, 0), w_far, swap(w_far, 1, 0)]

    query, key, value, chances, *mixed, normed = attention(me, blocks, gain_attn, w_qkv)
    heads = [mixed[0]] + [swap(mixed[k], k, 0) for k in range(1, 4)]
    mine, other = project(me, heads, weights)
    other = swap(other, 0, 1)
    hidden, tiles = send_hidden(me, ids, tokens, mine, other, experts)
    in_grads, in_upstream = experts_early(got_grads, w_down)
    tiles, in_grads = lax.optimization_barrier((tiles, in_grads))
    got_hidden = exchange(tiles)
    got_hidden, hidden = lax.optimization_barrier((got_hidden, hidden))
    hidden_other = swap(hidden, 0, 1)

    tiles, in_rows, *saved = experts_forward(got_hidden, in_upstream, gain_ffn, w_pair)
    got_back = exchange(tiles)
    grad_pair, grad_down = expert_grads(in_rows, in_grads, *saved)

    upstream = combine(ids, got_back, half)
    halves = (hidden, hidden_other, upstream, swap(upstream, 0, 1))
    grad_hidden, rounded, *grads = hidden_grad(
        me, grad_out, halves, gain_ffn, weights)
    grads = [grads[0]] + [swap(grads[k], k, 0) for k in range(1, 4)]
    all_grads = sequence(rounded, True)

    acts, near, far, near_out, far_out = attention_back(grads, query, key, value, chances, w_qkv)
    near_in = swap(near_out, 1, 0)
    far_in = swap(far_out, 1, 0)
    sent = weight_grads(acts, normed, mixed, all_grads, lax.axis_size("dp"))
    got = lax.all_to_all(sent, "dp", 0, 0, tiled=True)
    mine, near_other, far_mine, far_other = split_sums(me, near, near_in, far, far_in)
    arrived = (swap(near_other, 0, 1), swap(far_mine, 2, 0), swap(far_other, 2, 1))
    done = tokens_grad(me, mine, arrived, tokens, grad_hidden, gain_attn)
    done_other = swap(done, 0, 1)
    grad_tokens = join(me, done, done_other)
    grad_qkv, grad_attn_out = weight_sum(got)
    return (grad_tokens, grad_qkv, grad_attn_out, grad_pair.transpose(0, 1, 3, 2), grad_down)


def solution(mesh):
    return jax.shard_map(
        body,
        mesh=mesh,
        in_specs=(
            P(("dp", "head"), None),
            P(("dp", "head"), None),
            P(None, None, ("head", "group")),
            P(("head", "group"), None),
            P(),
            P(),
            P(("dp", "head"), None, None, "group"),
            P(("dp", "head"), "group", None),
            P(("dp", "head"), None),
            P(("dp", "head"), None),
        ),
        out_specs=(
            P(("dp", "head"), None),
            P(None, "dp", ("head", "group")),
            P(("head", "group"), "dp"),
            P(("dp", "head"), None, None, "group"),
            P(("dp", "head"), "group", None),
        ),
        check_vma=False,
    )
```
